128 devices in a mesh: lon: 32 (over z, x, core), lat: 4 (over y).
Axes of the slice: x: 4, y: 4, z: 4, core: 2. Of those that a mesh axis runs over, the one named last changes fastest.
Arguments:
- fields: bfloat16 [222, 512, 512], P(None, 'lon', 'lat'), may hold values from -6 to 6
- conv_weight: bfloat16 [9, 128, 222], replicated, may hold values from -0.125 to 0.125
- regrid_blocks: bfloat16 [16384, 128, 128], P(('lon', 'lat')), may hold values from -0.125 to 0.125
- source_block: int32 [16384], P(('lon', 'lat')), may hold values from 0 to 15
- target_device: int32 [16384, 1], replicated, may hold values from 0 to 127; in each aligned block of 128 rows (0 to 127, 128 to 255, ...) at most 2 rows name the same one
- target_half: int32 [16384], replicated, may hold values from 0 to 7
- neighbours: int32 [512, 4, 3], P(('lon', 'lat')), may hold values from 0 to 511, as said below
- hp_weight: bfloat16 [2, 128, 128], replicated, may hold values from -0.3125 to 0.3125
- rate_scale: float32 [128], replicated, may hold values from 0.3 to 3
Outputs:
- latent_codes: bfloat16 [131072, 128], P(('lon', 'lat'))
- grad_fields: float32 [222, 512, 512], P(None, 'lon', 'lat')
The draws below stay inside these ranges and needn't reach their ends.
Inputs may be any that keep to these rules, and one draw needn't show every extreme that they name: `target_device`: within the 128 blocks of one device no device is named more than 2 times, and some device is named exactly 2 times. `neighbours`: entries are (tile, side, reversed). Side 0 meets side 2 and side 1 meets side 3; the relation is symmetric with the same reversal bit on both sides of a pair. Across side 0 or 2 the neighbour lies on a device whose lon index is one above or one below around the cycle (side 0 above); across side 1 or 3 on a device with the same lon index.
All inputs are finite; a program needn't handle non-finite values.
Results may differ from the reference program's by a relative error of at most 0.008.
Values may be sent and summed in bfloat16 or wider, within the bound.
A program may use at most 128 MiB of HBM per device.

```python
import math
import jax
import jax.numpy as jnp
import numpy as np
from jax import lax

CIN = 222
LC = 128
TS = 16
BLK = 128
CAP = 2
NB = 128
LATD = 128
LOND = 16
TILES_DEV = 4
NLON = 512
NLAT = 512
SRCB = 16
HT_DEV = 8
NTILES = 512
NPIX = 131072
NBLOCKS = 16384
N_LON = 32
N_LAT = 4
DEVICES = 128


def draw_neighbours(key, part):
    column_tiles = N_LAT * TILES_DEV
    sub_keys = jax.random.split(jax.random.fold_in(key, 11), 4)
    cycle_perm = jax.vmap(lambda sub_key: jax.random.permutation(sub_key, column_tiles))(jax.random.split(sub_keys[0], N_LON)).astype(jnp.int32)
    band_perm = jax.vmap(lambda sub_key: jax.random.permutation(sub_key, column_tiles))(jax.random.split(sub_keys[1], N_LON)).astype(jnp.int32)
    cycle_flip = jax.random.randint(sub_keys[2], (N_LON, column_tiles), 0, 2).astype(jnp.int32)
    band_flip = jax.random.randint(sub_keys[3], (N_LON, column_tiles), 0, 2).astype(jnp.int32)
    positions = jnp.arange(column_tiles, dtype=jnp.int32)
    cycle_inverse = jax.vmap(lambda ordering: jnp.zeros((column_tiles,), jnp.int32).at[ordering].set(positions))(cycle_perm)
    band_inverse = jax.vmap(lambda ordering: jnp.zeros((column_tiles,), jnp.int32).at[ordering].set(positions))(band_perm)
    columns = jnp.arange(N_LON, dtype=jnp.int32)[:, None]
    next_col = (columns + 1) % N_LON
    prev_col = (columns - 1) % N_LON
    prev_inverse = cycle_inverse[prev_col[:, 0]]
    side_zero = next_col * column_tiles + cycle_perm
    side_two = prev_col * column_tiles + prev_inverse
    flip_two = jnp.take_along_axis(cycle_flip[prev_col[:, 0]], prev_inverse, axis=1)
    side_one = columns * column_tiles + band_perm
    side_three = columns * column_tiles + band_inverse
    flip_three = jnp.take_along_axis(band_flip, band_inverse, axis=1)
    tiles_out = jnp.stack([side_zero, side_one, side_two, side_three], -1)
    sides_out = jnp.broadcast_to(jnp.array([2, 3, 0, 1], jnp.int32), tiles_out.shape)
    flips_out = jnp.stack([cycle_flip, band_flip, flip_two, flip_three], -1)
    return jnp.stack([tiles_out, sides_out, flips_out], -1).reshape(N_LON * column_tiles, 4, 3).astype(jnp.int32)


def touch_ends(values, stream_key, smallest, high):
    place = [jax.random.randint(jax.random.fold_in(stream_key, axis), (), 0, length) for axis, length in enumerate(values.shape)]
    main_axis = values.shape.index(max(values.shape))
    neighbour = place[:main_axis] + [(place[main_axis] + 1) % values.shape[main_axis]] + place[main_axis + 1:]
    return values.at[tuple(place)].set(smallest).at[tuple(neighbour)].set(high)


def block_scale(stream_key, extent, cuts, least, top_value):
    def one(axis_at, shards_of):
        draws = jax.random.uniform(jax.random.fold_in(jax.random.fold_in(stream_key, 6), axis_at), (shards_of,), jnp.float32, least / len(cuts), top_value / len(cuts))
        return jnp.repeat(jnp.exp(draws), extent[axis_at] // shards_of).reshape((-1,) + (1,) * (len(extent) - axis_at - 1))

    loudness = one(*cuts[0])
    for cut in cuts[1:]:
        loudness = loudness * one(*cut)
    return loudness


def assign_block(stream_key, own, number, rows, count, top, most, skew):
    ranking = jax.random.permutation(stream_key, count)
    packed, ordinary = load_shares(count, rows * top, most, skew, True), load_shares(count, rows * top, most, skew, False)
    places = jnp.arange(count)

    def named(lengths, offset_by):
        used = int((lengths > 0).sum())
        fixed = max(1, used // 4)
        shifted = fixed + (places - fixed + offset_by * (used - fixed)) % max(1, count - fixed)
        return jnp.zeros((count,), jnp.int32).at[ranking[jnp.where(places < fixed, places, shifted)]].set(jnp.asarray(lengths, jnp.int32))

    lengths = jnp.where(number % 4 == 0, named(packed, number // 4), named(ordinary, number - number // 4 - 1))
    mixed = jax.random.permutation(jax.random.fold_in(own, 3), count)
    giver, receiver = mixed[0:count // 2 * 2:2], mixed[1:count // 2 * 2:2]
    room = jnp.minimum(lengths[giver] - 1, most - lengths[receiver]) // 2
    room = jnp.where((giver == ranking[0]) | (receiver == ranking[0]) | (lengths[receiver] == 0), 0, jnp.maximum(room, 0))
    shifted = jax.random.randint(jax.random.fold_in(own, 4), (count // 2,), 0, 1 << 20) % (room + 1)
    lengths = lengths.at[giver].add(-shifted).at[receiver].add(shifted)
    labels = jnp.searchsorted(jnp.cumsum(lengths), jnp.arange(rows * top), side="right").astype(jnp.int32)
    table = labels.reshape(top, rows).T
    table = table[jax.random.permutation(jax.random.fold_in(own, 1), rows)]
    offset_by = jax.random.randint(jax.random.fold_in(own, 2), (rows, 1), 0, top)
    return jnp.take_along_axis(table, (jnp.arange(top)[None, :] + offset_by) % top, axis=1)


def load_shares(count, total, limit, skew, full):
    loads = [(1 << 20) // math.isqrt(grade ** skew) + 1 for grade in range(1, count + 1)]
    largest = limit if full else min(limit, max(-(-total // count), total * loads[0] // sum(loads)))
    least = 1 if total - largest >= count - 1 else 0
    counts, spare = [largest] + [least] * (count - 1), total - largest - least * (count - 1)
    while spare > 0:
        movable = [i for i in range(1, count) if counts[i] < largest] or [i for i in range(1, count) if counts[i] < limit]
        pool, remaining = sum([loads[i] for i in movable]), spare
        for i in movable:
            more = min(limit - counts[i], max(1, remaining * loads[i] // pool), spare)
            counts[i] = counts[i] + more
            spare = spare - more
    return np.array(counts)


def centred(key, dims, width, reach, cuts=(), held_as=jnp.bfloat16):
    gain = block_scale(key, dims, cuts, -0.22, 0.18) if cuts else 1.0
    values = jax.random.normal(key, dims, jnp.float32) * width * gain
    return jnp.minimum(jnp.maximum(values, -reach), reach).astype(held_as)


def setup_inputs(seed: int = 0) -> dict:
    keys = jax.random.split(jax.random.key(seed), 10)
    fields = centred(keys[0], (CIN, NLON, NLAT), 1.0, 6.0, ((1, 32), (2, 4)))
    conv_weight = centred(keys[1], (9, LC, CIN), (9 * CIN) ** -0.5, 0.125)
    regrid_blocks = centred(keys[2], (NBLOCKS, BLK, BLK), (BLK * max(1, NB // HT_DEV)) ** -0.5, 0.125, ((0, 128),))
    source_block = touch_ends(jax.random.randint(keys[3], (NBLOCKS,), 0, SRCB), jax.random.fold_in(keys[3], 1), 0, SRCB - 1).astype(jnp.int32)
    target_device_keys = jax.random.split(jax.random.fold_in(keys[4], 1), NBLOCKS // NB)
    target_device_turns = jax.random.permutation(jax.random.fold_in(keys[4], 3), NBLOCKS // NB)
    target_device = jax.vmap(lambda own, number: assign_block(jax.random.fold_in(keys[4], 2), own, number, NB, DEVICES, 1, CAP, 2))(target_device_keys, target_device_turns).reshape((NBLOCKS, 1))
    target_half = touch_ends(jax.random.randint(keys[5], (NBLOCKS,), 0, HT_DEV), jax.random.fold_in(keys[5], 1), 0, HT_DEV - 1).astype(jnp.int32)
    neighbours = draw_neighbours(jax.random.fold_in(keys[9], 71), 0)
    hp_weight = centred(keys[7], (2, LC, LC), (3 * LC) ** -0.5, 0.3125)
    rate_scale = jnp.clip(jnp.exp(jax.random.uniform(keys[8], (LC,), jnp.float32, math.log(0.3), math.log(3.0))), 0.3, 3.0)
    return dict(fields=fields, conv_weight=conv_weight, regrid_blocks=regrid_blocks, source_block=source_block, target_device=target_device, target_half=target_half, neighbours=neighbours, hp_weight=hp_weight, rate_scale=rate_scale)


LOG_TWO = 0.6931471805599453


def silu_slope(values):
    sigma = jax.nn.sigmoid(values)
    return sigma * (1.0 + values * (1.0 - sigma))


def laplace_slope(latent, spread):
    magnitude = jnp.abs(latent)
    edge_mass = jnp.exp(-0.5 / spread)
    near_mass = 1.0 - edge_mass * jnp.cosh(jnp.minimum(magnitude, 0.5) / spread)
    slope_near = edge_mass * jnp.sinh(jnp.clip(latent, -0.5, 0.5) / spread) / (spread * near_mass * LOG_TWO)
    slope_far = jnp.sign(latent) / (spread * LOG_TWO)
    return jnp.where(magnitude < 0.5, slope_near, slope_far)


def conv_taps(kernel, padded, reverse):
    lon_cells = padded.shape[1] - 2
    lat_cells = padded.shape[2] - 2
    out_rows = kernel.shape[2] if reverse else kernel.shape[1]
    result = jnp.zeros((out_rows, lon_cells * lat_cells), jnp.float32)
    for tap_index in range(9):
        lon_shift = tap_index // 3
        lat_shift = tap_index % 3
        if reverse:
            lon_shift = 2 - lon_shift
            lat_shift = 2 - lat_shift
        window = padded[:, lon_shift:lon_shift + lon_cells, lat_shift:lat_shift + lat_cells].reshape(padded.shape[0], lon_cells * lat_cells)
        if reverse:
            result = result + lax.dot_general(kernel[tap_index], window, (((0,), (0,)), ((), ())), preferred_element_type=jnp.float32)
        else:
            result = result + jnp.dot(kernel[tap_index], window, preferred_element_type=jnp.float32)
    return result


def tile_edges(tile_values):
    return jnp.stack([tile_values[:, 0], tile_values[:, :, -1], tile_values[:, -1], tile_values[:, :, 0]], axis=1)


def neighbour_sum(tile_values, rim_values):
    tiles_float = tile_values.astype(jnp.float32)
    from_above = jnp.concatenate([rim_values[:, 0][:, None], tiles_float[:, :-1]], axis=1)
    from_below = jnp.concatenate([tiles_float[:, 1:], rim_values[:, 2][:, None]], axis=1)
    from_left = jnp.concatenate([rim_values[:, 3][:, :, None], tiles_float[:, :, :-1]], axis=2)
    from_right = jnp.concatenate([tiles_float[:, :, 1:], rim_values[:, 1][:, :, None]], axis=2)
    return from_above + from_below + from_left + from_right


def gather_rims(edge_rows, neighbours):
    straight = edge_rows[neighbours[:, :, 0], neighbours[:, :, 1]]
    flipped = straight[:, :, ::-1]
    return jnp.where(neighbours[:, :, 2][:, :, None, None] == 1, flipped, straight).astype(jnp.float32)


def cycle_pad(values):
    wrapped = jnp.concatenate([values[:, -1:], values, values[:, :1]], axis=1)
    return jnp.pad(wrapped, ((0, 0), (0, 0), (1, 1)))


def reference(fields, conv_weight, regrid_blocks, source_block, target_device, target_half, neighbours, hp_weight, rate_scale):
    device_count = N_LON * N_LAT
    pre_conv = conv_taps(conv_weight, cycle_pad(fields), False)
    hidden = jax.nn.silu(pre_conv).astype(jnp.bfloat16)
    by_device = hidden.reshape(LC, N_LON, LOND, N_LAT, LATD).transpose(1, 3, 0, 2, 4).reshape(device_count, LC, SRCB, BLK)
    owner = jnp.arange(NBLOCKS, dtype=jnp.int32) // NB
    sources = by_device[owner, :, source_block]
    contrib = jnp.einsum("bij,bcj->bic", regrid_blocks.astype(jnp.float32), sources.astype(jnp.float32), precision=lax.Precision.HIGHEST).astype(jnp.bfloat16)
    destination = (target_device[:, 0] * HT_DEV + target_half).astype(jnp.int32)
    latent_in = jax.ops.segment_sum(contrib.astype(jnp.float32), destination, num_segments=NPIX // BLK).astype(jnp.bfloat16)
    latent_in = latent_in.reshape(NPIX, LC)
    tiles_in = latent_in.reshape(NTILES, TS, TS, LC)
    rim_values = gather_rims(tile_edges(tiles_in), neighbours)
    near_sum = neighbour_sum(tiles_in, rim_values).astype(jnp.bfloat16).reshape(NPIX, LC)
    pre_mix = jnp.dot(latent_in, hp_weight[0], preferred_element_type=jnp.float32) + jnp.dot(near_sum, hp_weight[1], preferred_element_type=jnp.float32)
    mixed_latent = jax.nn.silu(pre_mix)
    bit_slope = laplace_slope(mixed_latent, rate_scale)
    mix_grad = (bit_slope * silu_slope(pre_mix)).astype(jnp.bfloat16)
    self_grad = lax.dot_general(mix_grad, hp_weight[0], (((1,), (1,)), ((), ())), preferred_element_type=jnp.float32)
    near_grad = lax.dot_general(mix_grad, hp_weight[1], (((1,), (1,)), ((), ())), preferred_element_type=jnp.float32)
    near_grad = near_grad.astype(jnp.bfloat16).reshape(NTILES, TS, TS, LC)
    back_rims = gather_rims(tile_edges(near_grad), neighbours)
    latent_grad = (self_grad + neighbour_sum(near_grad, back_rims).reshape(NPIX, LC)).astype(jnp.bfloat16)
    contrib_grad = latent_grad.reshape(NPIX // BLK, BLK, LC)[destination]
    source_grad = jnp.einsum("bij,bic->bcj", regrid_blocks.astype(jnp.float32), contrib_grad.astype(jnp.float32), precision=lax.Precision.HIGHEST)
    hidden_grad = jax.ops.segment_sum(source_grad, (owner * SRCB + source_block).astype(jnp.int32), num_segments=device_count * SRCB)
    hidden_grad = hidden_grad.reshape(N_LON, N_LAT, SRCB, LC, BLK).transpose(3, 0, 1, 2, 4)
    hidden_grad = hidden_grad.reshape(LC, N_LON, N_LAT, LOND, LATD).transpose(0, 1, 3, 2, 4).reshape(LC, NLON * NLAT)
    pre_grad = (hidden_grad * silu_slope(pre_conv)).astype(jnp.bfloat16).reshape(LC, NLON, NLAT)
    grad_fields = conv_taps(conv_weight, cycle_pad(pre_grad), True).reshape(CIN, NLON, NLAT)
    return mixed_latent.astype(jnp.bfloat16), grad_fields
```

```python
import functools

import jax
import jax.numpy as jnp
from jax import lax
from jax.experimental import pallas as pl
from jax.experimental.pallas import tpu as pltpu
from jax.sharding import PartitionSpec as P

TS = 16
RING = 4
BLOCK = 128
HALVES = 8
MESH = pl.DeviceIdType.MESH
LOG_TWO = 0.6931471805599453

PARTS = ((0, 48), (48, 48), (96, 32))
LINE = ("y", "z", "x")
PLANE = (("z", "x"), ("x", "y"), ("y", "z"))


def extended(cells, sides, width):
    for axis, dim in sides:
        count = lax.axis_size(axis)
        head = lax.slice_in_dim(cells, 0, width, axis=dim)
        tail = lax.slice_in_dim(cells, cells.shape[dim] - width, cells.shape[dim], axis=dim)
        cells = jnp.concatenate(
            [
                lax.ppermute(tail, axis, [(i, (i + 1) % count) for i in range(count)]),
                cells,
                lax.ppermute(head, axis, [((i + 1) % count, i) for i in range(count)]),
            ],
            axis=dim,
        )
    return cells


def joined_along(parts, dim):
    parts = jnp.moveaxis(parts, 0, dim)
    shape = parts.shape
    return parts.reshape(*shape[:dim], shape[dim] * shape[dim + 1], *shape[dim + 2 :])


def from_everyone(x, axis):
    peers = lax.axis_size(axis)
    return lax.all_to_all(jnp.broadcast_to(x[None], (peers, *x.shape)), axis, 0, 0, tiled=True)


def collect(x, axis, dim):
    return joined_along(from_everyone(x, axis), dim)


def passed_along(value, axis, steps):
    count = lax.axis_size(axis)
    pairs = [(source, (source + steps) % count) for source in range(count)]
    return lax.ppermute(value, axis, pairs)


def silu_slope(values):
    sigma = jax.nn.sigmoid(values)
    return sigma * (1.0 + values * (1.0 - sigma))


def laplace_slope(latent, spread):
    magnitude = jnp.abs(latent)
    edge_mass = jnp.exp(-0.5 / spread)
    near_mass = 1.0 - edge_mass * jnp.cosh(jnp.minimum(magnitude, 0.5) / spread)
    slope_near = (
        edge_mass * jnp.sinh(jnp.clip(latent, -0.5, 0.5) / spread) / (spread * near_mass * LOG_TWO)
    )
    slope_far = jnp.sign(latent) / (spread * LOG_TWO)
    return jnp.where(magnitude < 0.5, slope_near, slope_far)


def conv_taps(kernel, padded, reverse):
    lon_cells = padded.shape[1] - 2
    lat_cells = padded.shape[2] - 2
    out_rows = kernel.shape[2] if reverse else kernel.shape[1]
    result = jnp.zeros((out_rows, lon_cells * lat_cells), jnp.float32)
    for tap_index in range(9):
        lon_shift = tap_index // 3
        lat_shift = tap_index % 3
        if reverse:
            lon_shift = 2 - lon_shift
            lat_shift = 2 - lat_shift
        window = padded[
            :, lon_shift : lon_shift + lon_cells, lat_shift : lat_shift + lat_cells
        ].reshape(padded.shape[0], lon_cells * lat_cells)
        if reverse:
            result = result + lax.dot_general(
                kernel[tap_index],
                window,
                (((0,), (0,)), ((), ())),
                preferred_element_type=jnp.float32,
            )
        else:
            result = result + jnp.dot(kernel[tap_index], window, preferred_element_type=jnp.float32)
    return result


def tile_edges(tile_values):
    return jnp.stack(
        [tile_values[:, 0], tile_values[:, :, -1], tile_values[:, -1], tile_values[:, :, 0]], axis=1
    )


def neighbour_sum(tile_values, rim_values):
    tiles_float = tile_values.astype(jnp.float32)
    from_above = jnp.concatenate([rim_values[:, 0][:, None], tiles_float[:, :-1]], axis=1)
    from_below = jnp.concatenate([tiles_float[:, 1:], rim_values[:, 2][:, None]], axis=1)
    from_left = jnp.concatenate([rim_values[:, 3][:, :, None], tiles_float[:, :, :-1]], axis=2)
    from_right = jnp.concatenate([tiles_float[:, :, 1:], rim_values[:, 1][:, :, None]], axis=2)
    return from_above + from_below + from_left + from_right


def grid_rims(values):
    padded = extended(values, (("lon", 1), ("lat", 2)), 1)
    lat_pos = lax.axis_index("lat")
    lat_last = lax.axis_size("lat") - 1
    column = lax.broadcasted_iota(jnp.int32, (1, 1, padded.shape[2]), 2)
    outside = (column == 0) & (lat_pos == 0) | (column == padded.shape[2] - 1) & (
        lat_pos == lat_last
    )
    return jnp.where(outside, jnp.zeros_like(padded), padded)


def pick_rims(edge_rows, tile_pos, side_pos, flip_bit):
    tile_count = edge_rows.shape[0]
    flat_edges = edge_rows.reshape(tile_count * 4, -1)
    flipped = edge_rows[:, :, ::-1, :].reshape(tile_count * 4, -1)
    target_column = (tile_pos * 4 + side_pos)[..., None]
    column_ids = jnp.arange(tile_count * 4, dtype=jnp.int32)
    straight = (
        ((target_column == column_ids) & (flip_bit[..., None] == 0))
        .astype(jnp.bfloat16)
        .reshape(-1, tile_count * 4)
    )
    reversed_pick = (
        ((target_column == column_ids) & (flip_bit[..., None] == 1))
        .astype(jnp.bfloat16)
        .reshape(-1, tile_count * 4)
    )
    picked = jnp.dot(straight, flat_edges, preferred_element_type=jnp.float32) + jnp.dot(
        reversed_pick, flipped, preferred_element_type=jnp.float32
    )
    return picked.reshape(tile_pos.shape + edge_rows.shape[2:])


def fetch_rims(edge_rows, neighbours):
    band_edges = collect(edge_rows, "lat", 0)
    column_tiles = band_edges.shape[0]
    beside_all = []
    for step_by in (1, -1):
        beside_all.append(passed_along(band_edges, "lon", step_by))
    joined = jnp.concatenate([beside_all[0], band_edges, beside_all[1]], axis=0)
    owner_col = neighbours[:, :, 0] // column_tiles
    relative = (owner_col - lax.axis_index("lon") + 1) % lax.axis_size("lon")
    position = relative * column_tiles + neighbours[:, :, 0] % column_tiles
    return pick_rims(joined, position, neighbours[:, :, 1], neighbours[:, :, 2])


def torus_position():
    lon = lax.axis_index("lon")
    return {"z": lon // 8, "x": (lon // 2) % 4, "c": lon % 2, "y": lax.axis_index("lat")}


def moved(here, **steps):
    place = dict(here)
    for axis, step in steps.items():
        if axis == "c":
            place["c"] = (here["c"] + step) % 2
        else:
            place[axis] = (here[axis] + step + RING) % RING
    return place


def device_at(place):
    return (place["z"] * 8 + place["x"] * 2 + place["c"], place["y"])


def meet(peers):
    barrier = pltpu.get_barrier_semaphore()
    for peer in peers:
        pl.semaphore_signal(barrier, inc=1, device_id=device_at(peer), device_id_type=MESH)
    pl.semaphore_wait(barrier, len(peers))


def line_body(sign, s0, s1, s2, r0, r1, r2, send, recv, local):
    here = torus_position()
    peers = [moved(here, c=1)]
    for axis in LINE:
        for step in range(1, RING):
            for flip in range(2):
                peers.append(moved(here, **{axis: step, "c": flip}))
    meet(peers)
    sources, targets = (s0, s1, s2), (r0, r1, r2)
    copies = []
    for chunk in (4, 5, 2, 3, 6, 7, 1):
        step, flip = chunk // 2, chunk % 2
        for k in range(3):
            copy = pltpu.make_async_remote_copy(
                src_ref=sources[k].at[chunk],
                dst_ref=targets[k].at[chunk],
                send_sem=send.at[k, chunk],
                recv_sem=recv.at[k, chunk],
                device_id=device_at(moved(here, **{LINE[k]: sign * step, "c": flip})),
                device_id_type=MESH,
            )
            copy.start()
            copies.append(copy)
    own = []
    for k in range(3):
        copy = pltpu.make_async_copy(sources[k].at[0], targets[k].at[0], local.at[k])
        copy.start()
        own.append(copy)
    for copy in own + copies:
        copy.wait()


def line_exchange(parts, sign, collective_id):
    anywhere = pl.BlockSpec(memory_space=pl.ANY)
    return pl.pallas_call(
        functools.partial(line_body, sign),
        out_shape=[jax.ShapeDtypeStruct(part.shape, part.dtype) for part in parts],
        in_specs=[anywhere] * 3,
        out_specs=[anywhere] * 3,
        scratch_shapes=[
            pltpu.SemaphoreType.DMA((3, 8)),
            pltpu.SemaphoreType.DMA((3, 8)),
            pltpu.SemaphoreType.DMA((3,)),
        ],
        compiler_params=pltpu.CompilerParams(collective_id=collective_id, has_side_effects=True),
        name="line_exchange_%d" % collective_id,
    )(*parts)


def plane_body(p0, p1, p2, q0, q1, q2, send, recv, local):
    here = torus_position()
    peers = []
    for axis in LINE:
        for step in range(1, RING):
            peers.append(moved(here, **{axis: step}))
    for first, second in PLANE:
        for step in range(1, RING):
            for other in range(1, RING):
                peers.append(moved(here, **{first: step, second: other}))
    meet(peers)
    sources, targets = (p0, p1, p2), (q0, q1, q2)
    copies = []
    for place in (10, 5, 15, 7, 13, 9, 11, 6, 14, 2, 8, 1, 3, 4, 12):
        for k in range(3):
            copy = pltpu.make_async_remote_copy(
                src_ref=sources[k].at[place],
                dst_ref=targets[k].at[place],
                send_sem=send.at[k, place],
                recv_sem=recv.at[k, place],
                device_id=device_at(
                    moved(here, **{PLANE[k][0]: place // RING, PLANE[k][1]: place % RING})
                ),
                device_id_type=MESH,
            )
            copy.start()
            copies.append(copy)
    own = []
    for k in range(3):
        copy = pltpu.make_async_copy(sources[k].at[0], targets[k].at[0], local.at[k])
        copy.start()
        own.append(copy)
    for copy in own + copies:
        copy.wait()


def plane_scatter(parts, collective_id):
    anywhere = pl.BlockSpec(memory_space=pl.ANY)
    return pl.pallas_call(
        plane_body,
        out_shape=[jax.ShapeDtypeStruct(part.shape, part.dtype) for part in parts],
        in_specs=[anywhere] * 3,
        out_specs=[anywhere] * 3,
        scratch_shapes=[
            pltpu.SemaphoreType.DMA((3, 16)),
            pltpu.SemaphoreType.DMA((3, 16)),
            pltpu.SemaphoreType.DMA((3,)),
        ],
        compiler_params=pltpu.CompilerParams(collective_id=collective_id, has_side_effects=True),
        name="plane_scatter",
    )(*parts)


def gather_body(grad, u0, u1, u2, send, recv, local):
    here = torus_position()
    peers = []
    for axis in LINE:
        for step in range(1, RING):
            peers.append(moved(here, **{axis: step}))
    meet(peers)
    targets = (u0, u1, u2)

    def sent(k, source, place, axis, step):
        copy = pltpu.make_async_remote_copy(
            src_ref=source,
            dst_ref=targets[k].at[place],
            send_sem=send.at[k, place],
            recv_sem=recv.at[k, place],
            device_id=device_at(moved(here, **{axis: -step})),
            device_id_type=MESH,
        )
        copy.start()
        return copy

    first, later = {}, []
    mine = [grad.at[:, pl.ds(start, count)] for start, count in PARTS]
    for step in (2, 1, 3):
        for k in range(3):
            first[k, step] = sent(k, mine[k], step, PLANE[k][1], step)
    for step in (2, 1, 3):
        for k in range(3):
            later.append(sent(k, mine[k], step * RING, PLANE[k][0], step))
    own = []
    for k in range(3):
        copy = pltpu.make_async_copy(mine[k], targets[k].at[0], local.at[k])
        copy.start()
        own.append(copy)
    for step in (1, 3, 2):
        for k in range(3):
            first[k, step].wait_recv()
            for hop in (2, 1, 3):
                later.append(sent(k, targets[k].at[step], hop * RING + step, PLANE[k][0], hop))
    for copy in own + later:
        copy.wait()
    for copy in first.values():
        copy.wait_send()


def plane_gather(grad, collective_id):
    anywhere = pl.BlockSpec(memory_space=pl.ANY)
    return pl.pallas_call(
        gather_body,
        out_shape=[
            jax.ShapeDtypeStruct((16, HALVES, count, grad.shape[2]), grad.dtype)
            for _, count in PARTS
        ],
        in_specs=[anywhere],
        out_specs=[anywhere] * 3,
        scratch_shapes=[
            pltpu.SemaphoreType.DMA((3, 16)),
            pltpu.SemaphoreType.DMA((3, 16)),
            pltpu.SemaphoreType.DMA((3,)),
        ],
        compiler_params=pltpu.CompilerParams(collective_id=collective_id, has_side_effects=True),
        name="plane_gather",
    )(grad)


def spread_body(table, hidden, blocks, o0, o1, o2, turned, stage, sems):
    step = pl.program_id(0)
    last = pl.num_programs(0) - 1
    slot = step % 2
    outs = (o0, o1, o2)

    def drained(which):
        pltpu.make_async_copy(stage.at[which], stage.at[which], sems.at[which]).wait()

    @pl.when(step == 0)
    def _():
        for k in range(turned.shape[0]):
            turned[k] = hidden[:, k * BLOCK : (k + 1) * BLOCK].T

    @pl.when(step >= 2)
    def _():
        drained(slot)

    for b in range(blocks.shape[0]):
        block = step * blocks.shape[0] + b
        stage[slot, b] = jnp.dot(
            blocks[b], turned[table[0, block]], preferred_element_type=jnp.float32
        ).astype(stage.dtype)
        for k, (start, count) in enumerate(PARTS):
            pltpu.make_async_copy(
                stage.at[slot, b, pl.ds(start, count)],
                outs[k].at[table[1 + 2 * k, block], table[2 + 2 * k, block]],
                sems.at[slot],
            ).start()

    @pl.when(step == last)
    def _():
        drained(1 - slot)
        drained(slot)


def spread(table, hidden, regrid_blocks):
    count, rows, cells = regrid_blocks.shape
    width = hidden.shape[0]
    group = 8
    return pl.pallas_call(
        spread_body,
        grid_spec=pltpu.PrefetchScalarGridSpec(
            num_scalar_prefetch=1,
            grid=(count // group,),
            in_specs=[
                pl.BlockSpec(hidden.shape, lambda i, t: (0, 0)),
                pl.BlockSpec((group, rows, cells), lambda i, t: (i, 0, 0)),
            ],
            out_specs=[pl.BlockSpec(memory_space=pl.ANY)] * 3,
            scratch_shapes=[
                pltpu.VMEM((hidden.shape[1] // BLOCK, cells, width), jnp.bfloat16),
                pltpu.VMEM((2, group, rows, width), jnp.bfloat16),
                pltpu.SemaphoreType.DMA((2,)),
            ],
        ),
        out_shape=[jax.ShapeDtypeStruct((8, 32, n, width), jnp.bfloat16) for _, n in PARTS],
        name="spread",
    )(table, hidden, regrid_blocks)


def source_and_place(spot, k, chunk, place):
    here = {"z": spot[0], "x": spot[1], "c": spot[2], "y": spot[3]}
    line = (here[LINE[k]] + RING - chunk // 2) % RING
    core = (here["c"] + chunk % 2) % 2
    source = core * RING + line if k == 0 else line * 2 + core
    first = (here[PLANE[k][0]] + place // RING) % RING
    second = (here[PLANE[k][1]] + place % RING) % RING
    return k * 256 + source * 32 + (first * RING + second) * 2


def combine_body(spot, table, r0, r1, r2, p0, p1, p2, a0, a1, a2):
    place = pl.program_id(0)
    ins, outs, sums = (r0, r1, r2), (p0, p1, p2), (a0, a1, a2)
    for total in sums:
        total[...] = jnp.zeros_like(total)
    for chunk in range(8):
        for k in range(3):
            entry = source_and_place(spot, k, chunk, place)
            for rank in range(2):
                half = table[entry + rank]
                sums[k][half] += ins[k][chunk, rank].astype(jnp.float32)
    for k in range(3):
        outs[k][0] = sums[k][:HALVES].astype(jnp.bfloat16)


def combine(spot, table, parts):
    width = parts[0].shape[-1]
    return pl.pallas_call(
        combine_body,
        grid_spec=pltpu.PrefetchScalarGridSpec(
            num_scalar_prefetch=2,
            grid=(16,),
            in_specs=[pl.BlockSpec((8, 2, n, width), lambda i, s, t: (0, i, 0, 0)) for _, n in PARTS],
            out_specs=[
                pl.BlockSpec((1, HALVES, n, width), lambda i, s, t: (i, 0, 0, 0)) for _, n in PARTS
            ],
            scratch_shapes=[pltpu.VMEM((HALVES + 1, n, width), jnp.float32) for _, n in PARTS],
        ),
        out_shape=[jax.ShapeDtypeStruct((16, HALVES, n, width), jnp.bfloat16) for _, n in PARTS],
        name="combine",
    )(spot, table, *parts)


def total_body(q0, q1, q2, out):
    for (start, count), part in zip(PARTS, (q0, q1, q2)):
        out[0, start : start + count] = jnp.sum(part[:, 0].astype(jnp.float32), axis=0).astype(
            out.dtype
        )


def total(parts):
    width = parts[0].shape[-1]
    return pl.pallas_call(
        total_body,
        grid=(HALVES,),
        in_specs=[pl.BlockSpec((16, 1, n, width), lambda i: (0, i, 0, 0)) for _, n in PARTS],
        out_specs=pl.BlockSpec((1, BLOCK, width), lambda i: (i, 0, 0)),
        out_shape=jax.ShapeDtypeStruct((HALVES, BLOCK, width), jnp.bfloat16),
        name="total",
    )(*parts)


def serve_body(spot, table, u0, u1, u2, v0, v1, v2):
    chunk = pl.program_id(0)
    ins, outs = (u0, u1, u2), (v0, v1, v2)
    for place in range(16):
        for k in range(3):
            entry = source_and_place(spot, k, chunk, place)
            for rank in range(2):
                half = jnp.minimum(table[entry + rank], HALVES - 1)
                outs[k][0, place * 2 + rank] = ins[k][place, half]


def serve(spot, table, parts):
    width = parts[0].shape[-1]
    return pl.pallas_call(
        serve_body,
        grid_spec=pltpu.PrefetchScalarGridSpec(
            num_scalar_prefetch=2,
            grid=(8,),
            in_specs=[
                pl.BlockSpec((16, HALVES, n, width), lambda i, s, t: (0, 0, 0, 0))
                for _, n in PARTS
            ],
            out_specs=[pl.BlockSpec((1, 32, n, width), lambda i, s, t: (i, 0, 0, 0)) for _, n in PARTS],
        ),
        out_shape=[jax.ShapeDtypeStruct((8, 32, n, width), jnp.bfloat16) for _, n in PARTS],
        name="serve",
    )(spot, table, *parts)


def pull_body(table, blocks, pre_conv, w0, w1, w2, out, stage, sums, sems):
    step = pl.program_id(0)
    steps = pl.num_programs(0)
    group = blocks.shape[0]
    slot = step % 2
    ins = (w0, w1, w2)

    def fetch(which, into):
        for b in range(group):
            block = which * group + b
            for k, (start, count) in enumerate(PARTS):
                pltpu.make_async_copy(
                    ins[k].at[table[1 + 2 * k, block], table[2 + 2 * k, block]],
                    stage.at[into, b, pl.ds(start, count)],
                    sems.at[into],
                ).start()

    @pl.when(step == 0)
    def _():
        fetch(0, 0)
        sums[...] = jnp.zeros_like(sums)

    @pl.when(step + 1 < steps)
    def _():
        fetch(step + 1, 1 - slot)

    pltpu.make_async_copy(stage.at[slot], stage.at[slot], sems.at[slot]).wait()
    for b in range(group):
        source = table[0, step * group + b]
        sums[source] += lax.dot_general(
            stage[slot, b],
            blocks[b],
            (((0,), (0,)), ((), ())),
            preferred_element_type=jnp.float32,
        )

    @pl.when(step + 1 == steps)
    def _():
        for k in range(sums.shape[0]):
            cells = slice(k * BLOCK, (k + 1) * BLOCK)
            out[:, cells] = (sums[k] * silu_slope(pre_conv[:, cells])).astype(out.dtype)


def pull(table, regrid_blocks, pre_conv, parts):
    count, rows, cells = regrid_blocks.shape
    width = pre_conv.shape[0]
    group = 8
    return pl.pallas_call(
        pull_body,
        grid_spec=pltpu.PrefetchScalarGridSpec(
            num_scalar_prefetch=1,
            grid=(count // group,),
            in_specs=[
                pl.BlockSpec((group, rows, cells), lambda i, t: (i, 0, 0)),
                pl.BlockSpec(pre_conv.shape, lambda i, t: (0, 0)),
            ]
            + [pl.BlockSpec(memory_space=pl.ANY)] * 3,
            out_specs=pl.BlockSpec(pre_conv.shape, lambda i, t: (0, 0)),
            scratch_shapes=[
                pltpu.VMEM((2, group, rows, width), jnp.bfloat16),
                pltpu.VMEM((pre_conv.shape[1] // BLOCK, width, cells), jnp.float32),
                pltpu.SemaphoreType.DMA((2,)),
            ],
        ),
        out_shape=jax.ShapeDtypeStruct(pre_conv.shape, jnp.bfloat16),
        name="pull",
    )(table, regrid_blocks, pre_conv, *parts)


def routing(source_block, target_device, target_half):
    here = torus_position()
    count = source_block.shape[0]

    def rows_of(values):
        grid = values.reshape(4, 4, 2, 4, count)
        picks = []
        for k in range(3):
            start = [here["z"], here["x"], 0, here["y"], 0]
            size = [1, 1, 2, 1, count]
            at = {"z": 0, "x": 1, "y": 3}[LINE[k]]
            start[at], size[at] = 0, 4
            picks.append(lax.dynamic_slice(grid, start, size).reshape(8, count))
        own = lax.dynamic_slice(
            grid, [here["z"], here["x"], here["c"], here["y"], 0], [1, 1, 1, 1, count]
        )
        return jnp.concatenate(picks + [own.reshape(1, count)], axis=0)

    targets = rows_of(target_device[:, 0])
    halves = rows_of(target_half)[:24]
    ids = jnp.arange(count, dtype=jnp.int32)
    rank = jnp.sum(
        (targets[:, :, None] == targets[:, None, :]) & (ids[None, None, :] < ids[None, :, None]),
        axis=2,
        dtype=jnp.int32,
    )
    to = {"z": targets // 32, "x": (targets // 8) % 4, "c": (targets // 4) % 2, "y": targets % 4}
    codes = []
    for k in range(3):
        rows = slice(8 * k, 8 * k + 8)
        fits = (to["c"][rows] == here["c"]) & (to[LINE[k]][rows] == here[LINE[k]])
        code = (to[PLANE[k][0]][rows] * RING + to[PLANE[k][1]][rows]) * 2 + rank[rows]
        codes.append(jnp.where(fits, code, -1))
    codes = jnp.concatenate(codes, axis=0)
    slots = jnp.arange(32, dtype=jnp.int32)
    table = HALVES + jnp.sum(
        jnp.where(codes[:, None, :] == slots[None, :, None], (halves - HALVES)[:, None, :], 0),
        axis=2,
    )
    own = {axis: value[24] for axis, value in to.items()}
    away = {axis: (own[axis] - here[axis] + RING) % RING for axis in ("z", "x", "y")}
    flip = (own["c"] + here["c"]) % 2
    lines = [source_block]
    for k in range(3):
        lines.append(away[LINE[k]] * 2 + flip)
        lines.append((away[PLANE[k][0]] * RING + away[PLANE[k][1]]) * 2 + rank[24])
    spot = jnp.stack([here["z"], here["x"], here["c"], here["y"]]).astype(jnp.int32)
    return spot, table.reshape(-1), jnp.stack(lines)


def on_device(
    fields,
    conv_weight,
    regrid_blocks,
    source_block,
    target_device,
    target_half,
    neighbours,
    hp_weight,
    rate_scale,
):
    channels, lon_cells, lat_cells = fields.shape
    latent_width = conv_weight.shape[1]
    tile_count = neighbours.shape[0]
    spot, table, lines = routing(source_block, target_device, target_half)
    pre_conv = conv_taps(conv_weight, grid_rims(fields), False)
    hidden = jax.nn.silu(pre_conv).astype(jnp.bfloat16)
    outgoing = spread(lines, hidden, regrid_blocks)
    arrived = line_exchange(outgoing, 1, 0)
    partial = combine(spot, table, arrived)
    latent_in = total(plane_scatter(partial, 1))
    tiles_in = latent_in.reshape(tile_count, TS, TS, latent_width)
    flat_latent = latent_in.reshape(-1, latent_width)
    rim_values = fetch_rims(tile_edges(tiles_in), neighbours)
    near_sum = neighbour_sum(tiles_in, rim_values).astype(jnp.bfloat16).reshape(-1, latent_width)
    pre_mix = jnp.dot(flat_latent, hp_weight[0], preferred_element_type=jnp.float32) + jnp.dot(
        near_sum, hp_weight[1], preferred_element_type=jnp.float32
    )
    mixed_latent = jax.nn.silu(pre_mix)
    bit_slope = laplace_slope(mixed_latent, rate_scale)
    mix_grad = (bit_slope * silu_slope(pre_mix)).astype(jnp.bfloat16)
    self_grad = lax.dot_general(
        mix_grad, hp_weight[0], (((1,), (1,)), ((), ())), preferred_element_type=jnp.float32
    )
    near_grad = lax.dot_general(
        mix_grad, hp_weight[1], (((1,), (1,)), ((), ())), preferred_element_type=jnp.float32
    )
    near_grad = near_grad.astype(jnp.bfloat16).reshape(tiles_in.shape)
    back_rims = fetch_rims(tile_edges(near_grad), neighbours)
    latent_grad = (
        self_grad + neighbour_sum(near_grad, back_rims).reshape(-1, latent_width)
    ).astype(jnp.bfloat16)
    halves_grad = latent_grad.reshape(HALVES, BLOCK, latent_width)
    replies = serve(spot, table, plane_gather(halves_grad, 2))
    answers = line_exchange(replies, -1, 3)
    pre_grad = pull(lines, regrid_blocks, pre_conv, answers).reshape(
        latent_width, lon_cells, lat_cells
    )
    grad_fields = conv_taps(conv_weight, grid_rims(pre_grad), True).reshape(
        channels, lon_cells, lat_cells
    )
    return (mixed_latent.astype(jnp.bfloat16), grad_fields)


def solution(mesh):
    placed = (
        P(None, "lon", "lat"),
        P(),
        P(("lon", "lat"), None, None),
        P(("lon", "lat")),
        P(),
        P(),
        P(("lon", "lat"), None, None),
        P(),
        P(),
    )
    return jax.shard_map(
        on_device,
        mesh=mesh,
        in_specs=placed,
        out_specs=(P(("lon", "lat"), None), P(None, "lon", "lat")),
        check_vma=False,
    )
```

```python
import functools

import jax
import jax.numpy as jnp
from jax import lax
from jax.experimental import pallas as pl
from jax.experimental.pallas import tpu as pltpu
from jax.sharding import PartitionSpec as P

TS = 16
RING = 4
BLOCK = 128
HALVES = 8
GROUP = 8
MESH = pl.DeviceIdType.MESH
LOG_TWO = 0.6931471805599453

PARTS = ((0, 48), (48, 48), (96, 32))
LINE = ("y", "z", "x")
PLANE = (("z", "x"), ("x", "y"), ("y", "z"))


def extended(cells, sides, width):
    for axis, dim in sides:
        count = lax.axis_size(axis)
        head = lax.slice_in_dim(cells, 0, width, axis=dim)
        tail = lax.slice_in_dim(cells, cells.shape[dim] - width, cells.shape[dim], axis=dim)
        cells = jnp.concatenate(
            [
                lax.ppermute(tail, axis, [(i, (i + 1) % count) for i in range(count)]),
                cells,
                lax.ppermute(head, axis, [((i + 1) % count, i) for i in range(count)]),
            ],
            axis=dim,
        )
    return cells


def silu_slope(values):
    sigma = jax.nn.sigmoid(values)
    return sigma * (1.0 + values * (1.0 - sigma))


def laplace_slope(latent, spread):
    magnitude = jnp.abs(latent)
    edge_mass = jnp.exp(-0.5 / spread)
    scaled = jnp.clip(latent, -0.5, 0.5) / spread
    grown, shrunk = jnp.exp(scaled), jnp.exp(-scaled)
    near_mass = 1.0 - edge_mass * (0.5 * (grown + shrunk))
    slope_near = edge_mass * (0.5 * (grown - shrunk)) / (spread * near_mass * LOG_TWO)
    side = jnp.where(latent > 0.0, 1.0, jnp.where(latent < 0.0, -1.0, 0.0))
    return jnp.where(magnitude < 0.5, slope_near, side / (spread * LOG_TWO))


def conv_taps(kernel, padded, reverse):
    lon_cells = padded.shape[1] - 2
    lat_cells = padded.shape[2] - 2
    out_rows = kernel.shape[2] if reverse else kernel.shape[1]
    result = jnp.zeros((out_rows, lon_cells * lat_cells), jnp.float32)
    for tap_index in range(9):
        lon_shift = tap_index // 3
        lat_shift = tap_index % 3
        if reverse:
            lon_shift = 2 - lon_shift
            lat_shift = 2 - lat_shift
        window = padded[
            :, lon_shift : lon_shift + lon_cells, lat_shift : lat_shift + lat_cells
        ].reshape(padded.shape[0], lon_cells * lat_cells)
        if reverse:
            result = result + lax.dot_general(
                kernel[tap_index],
                window,
                (((0,), (0,)), ((), ())),
                preferred_element_type=jnp.float32,
            )
        else:
            result = result + jnp.dot(kernel[tap_index], window, preferred_element_type=jnp.float32)
    return result


def grid_rims(values):
    padded = extended(values, (("lon", 1), ("lat", 2)), 1)
    lat_pos = lax.axis_index("lat")
    lat_last = lax.axis_size("lat") - 1
    column = lax.broadcasted_iota(jnp.int32, (1, 1, padded.shape[2]), 2)
    outside = (column == 0) & (lat_pos == 0) | (column == padded.shape[2] - 1) & (
        lat_pos == lat_last
    )
    return jnp.where(outside, jnp.zeros_like(padded), padded)


def torus_position():
    lon = lax.axis_index("lon")
    return {"z": lon // 8, "x": (lon // 2) % 4, "c": lon % 2, "y": lax.axis_index("lat")}


def moved(here, **steps):
    place = dict(here)
    for axis, step in steps.items():
        if axis == "c":
            place["c"] = (here["c"] + step) % 2
        else:
            place[axis] = (here[axis] + step + RING) % RING
    return place


def device_at(place):
    return (place["z"] * 8 + place["x"] * 2 + place["c"], place["y"])


def meet(peers):
    barrier = pltpu.get_barrier_semaphore()
    for peer in peers:
        pl.semaphore_signal(barrier, inc=1, device_id=device_at(peer), device_id_type=MESH)
    pl.semaphore_wait(barrier, len(peers))


def line_body(sign, s0, s1, s2, r0, r1, r2, send, recv, local):
    here = torus_position()
    peers = [moved(here, c=1)]
    for axis in LINE:
        for step in range(1, RING):
            for flip in range(2):
                peers.append(moved(here, **{axis: step, "c": flip}))
    meet(peers)
    sources, targets = (s0, s1, s2), (r0, r1, r2)
    copies = []
    for chunk in (4, 5, 2, 3, 6, 7, 1):
        step, flip = chunk // 2, chunk % 2
        for k in range(3):
            copy = pltpu.make_async_remote_copy(
                src_ref=sources[k].at[chunk],
                dst_ref=targets[k].at[chunk],
                send_sem=send.at[k, chunk],
                recv_sem=recv.at[k, chunk],
                device_id=device_at(moved(here, **{LINE[k]: sign * step, "c": flip})),
                device_id_type=MESH,
            )
            copy.start()
            copies.append(copy)
    own = []
    for k in range(3):
        copy = pltpu.make_async_copy(sources[k].at[0], targets[k].at[0], local.at[k])
        copy.start()
        own.append(copy)
    for copy in own + copies:
        copy.wait()


def line_exchange(parts, sign, collective_id):
    anywhere = pl.BlockSpec(memory_space=pl.ANY)
    return pl.pallas_call(
        functools.partial(line_body, sign),
        out_shape=[jax.ShapeDtypeStruct(part.shape, part.dtype) for part in parts],
        in_specs=[anywhere] * 3,
        out_specs=[anywhere] * 3,
        scratch_shapes=[
            pltpu.SemaphoreType.DMA((3, 8)),
            pltpu.SemaphoreType.DMA((3, 8)),
            pltpu.SemaphoreType.DMA((3,)),
        ],
        compiler_params=pltpu.CompilerParams(collective_id=collective_id, has_side_effects=True, vmem_limit_bytes=4 << 20),
        name="line_exchange_%d" % collective_id,
    )(*parts)


def plane_body(p0, p1, p2, q0, q1, q2, send, recv, local):
    here = torus_position()
    peers = []
    for axis in LINE:
        for step in range(1, RING):
            peers.append(moved(here, **{axis: step}))
    for first, second in PLANE:
        for step in range(1, RING):
            for other in range(1, RING):
                peers.append(moved(here, **{first: step, second: other}))
    meet(peers)
    sources, targets = (p0, p1, p2), (q0, q1, q2)
    copies = []
    for place in (10, 5, 15, 7, 13, 9, 11, 6, 14, 2, 8, 1, 3, 4, 12):
        for k in range(3):
            copy = pltpu.make_async_remote_copy(
                src_ref=sources[k].at[place],
                dst_ref=targets[k].at[place],
                send_sem=send.at[k, place],
                recv_sem=recv.at[k, place],
                device_id=device_at(
                    moved(here, **{PLANE[k][0]: place // RING, PLANE[k][1]: place % RING})
                ),
                device_id_type=MESH,
            )
            copy.start()
            copies.append(copy)
    own = []
    for k in range(3):
        copy = pltpu.make_async_copy(sources[k].at[0], targets[k].at[0], local.at[k])
        copy.start()
        own.append(copy)
    for copy in own + copies:
        copy.wait()


def plane_scatter(parts, collective_id):
    anywhere = pl.BlockSpec(memory_space=pl.ANY)
    return pl.pallas_call(
        plane_body,
        out_shape=[jax.ShapeDtypeStruct(part.shape, part.dtype) for part in parts],
        in_specs=[anywhere] * 3,
        out_specs=[anywhere] * 3,
        scratch_shapes=[
            pltpu.SemaphoreType.DMA((3, 16)),
            pltpu.SemaphoreType.DMA((3, 16)),
            pltpu.SemaphoreType.DMA((3,)),
        ],
        compiler_params=pltpu.CompilerParams(collective_id=collective_id, has_side_effects=True, vmem_limit_bytes=4 << 20),
        name="plane_scatter",
    )(*parts)


def gather_body(grad, u0, u1, u2, send, recv, local):
    here = torus_position()
    peers = []
    for axis in LINE:
        for step in range(1, RING):
            peers.append(moved(here, **{axis: step}))
    meet(peers)
    targets = (u0, u1, u2)

    def sent(k, source, place, axis, step):
        copy = pltpu.make_async_remote_copy(
            src_ref=source,
            dst_ref=targets[k].at[place],
            send_sem=send.at[k, place],
            recv_sem=recv.at[k, place],
            device_id=device_at(moved(here, **{axis: -step})),
            device_id_type=MESH,
        )
        copy.start()
        return copy

    first, later = {}, []
    mine = [grad.at[:, pl.ds(start, count)] for start, count in PARTS]
    for step in (2, 1, 3):
        for k in range(3):
            first[k, step] = sent(k, mine[k], step, PLANE[k][1], step)
    for step in (2, 1, 3):
        for k in range(3):
            later.append(sent(k, mine[k], step * RING, PLANE[k][0], step))
    own = []
    for k in range(3):
        copy = pltpu.make_async_copy(mine[k], targets[k].at[0], local.at[k])
        copy.start()
        own.append(copy)
    for step in (1, 3, 2):
        for k in range(3):
            first[k, step].wait_recv()
            for hop in (2, 1, 3):
                later.append(sent(k, targets[k].at[step], hop * RING + step, PLANE[k][0], hop))
    for copy in own + later:
        copy.wait()
    for copy in first.values():
        copy.wait_send()


def plane_gather(grad, collective_id):
    anywhere = pl.BlockSpec(memory_space=pl.ANY)
    return pl.pallas_call(
        gather_body,
        out_shape=[
            jax.ShapeDtypeStruct((16, HALVES, count, grad.shape[2]), grad.dtype)
            for _, count in PARTS
        ],
        in_specs=[anywhere],
        out_specs=[anywhere] * 3,
        scratch_shapes=[
            pltpu.SemaphoreType.DMA((3, 16)),
            pltpu.SemaphoreType.DMA((3, 16)),
            pltpu.SemaphoreType.DMA((3,)),
        ],
        compiler_params=pltpu.CompilerParams(collective_id=collective_id, has_side_effects=True, vmem_limit_bytes=4 << 20),
        name="plane_gather",
    )(grad)


def spread_body(table, hidden, blocks, o0, o1, o2, turned):
    outs = (o0, o1, o2)
    for k in range(turned.shape[0]):
        turned[k] = hidden[:, k * BLOCK : (k + 1) * BLOCK].T

    def some(step, carry):
        for b in range(GROUP):
            block = step * GROUP + b
            made = jnp.dot(
                blocks[block], turned[table[0, block]], preferred_element_type=jnp.float32
            ).astype(jnp.bfloat16)
            for k, (start, count) in enumerate(PARTS):
                outs[k][table[1 + k, block]] = made[start : start + count]
        return carry

    lax.fori_loop(0, blocks.shape[0] // GROUP, some, 0)


def spread(table, hidden, regrid_blocks):
    cells, width = regrid_blocks.shape[2], hidden.shape[0]
    vmem = pl.BlockSpec(memory_space=pltpu.VMEM)
    parts = pl.pallas_call(
        spread_body,
        in_specs=[pl.BlockSpec(memory_space=pltpu.SMEM), vmem, vmem],
        out_specs=[vmem] * 3,
        scratch_shapes=[pltpu.VMEM((hidden.shape[1] // BLOCK, cells, width), jnp.bfloat16)],
        out_shape=[jax.ShapeDtypeStruct((256, n, width), jnp.bfloat16) for _, n in PARTS],
        compiler_params=pltpu.CompilerParams(vmem_limit_bytes=24 << 20),
        name="spread",
    )(table, hidden, regrid_blocks)
    return [part.reshape(8, 32, *part.shape[1:]) for part in parts]


def combine_body(table, r0, r1, r2, p0, p1, p2, a0, a1, a2):
    place = pl.program_id(0)
    ins, outs, sums = (r0, r1, r2), (p0, p1, p2), (a0, a1, a2)
    for total in sums:
        total[...] = jnp.zeros_like(total)
    for chunk in range(8):
        for k in range(3):
            entry = k * 256 + chunk * 32 + place * 2
            for rank in range(2):
                half = table[entry + rank]
                sums[k][half] += ins[k][chunk, rank].astype(jnp.float32)
    for k in range(3):
        outs[k][0] = sums[k][:HALVES].astype(jnp.bfloat16)


def combine(table, parts):
    width = parts[0].shape[-1]
    return pl.pallas_call(
        combine_body,
        grid_spec=pltpu.PrefetchScalarGridSpec(
            num_scalar_prefetch=1,
            grid=(16,),
            in_specs=[pl.BlockSpec((8, 2, n, width), lambda i, t: (0, i, 0, 0)) for _, n in PARTS],
            out_specs=[
                pl.BlockSpec((1, HALVES, n, width), lambda i, t: (i, 0, 0, 0)) for _, n in PARTS
            ],
            scratch_shapes=[pltpu.VMEM((HALVES + 1, n, width), jnp.float32) for _, n in PARTS],
        ),
        out_shape=[jax.ShapeDtypeStruct((16, HALVES, n, width), jnp.bfloat16) for _, n in PARTS],
        compiler_params=pltpu.CompilerParams(vmem_limit_bytes=8 << 20),
        name="combine",
    )(table, *parts)


def total_body(q0, q1, q2, out):
    for (start, count), part in zip(PARTS, (q0, q1, q2)):
        out[0, start : start + count] = jnp.sum(part[:, 0].astype(jnp.float32), axis=0).astype(
            out.dtype
        )


def total(parts):
    width = parts[0].shape[-1]
    return pl.pallas_call(
        total_body,
        grid=(HALVES,),
        in_specs=[pl.BlockSpec((16, 1, n, width), lambda i: (0, i, 0, 0)) for _, n in PARTS],
        out_specs=pl.BlockSpec((1, BLOCK, width), lambda i: (i, 0, 0)),
        out_shape=jax.ShapeDtypeStruct((HALVES, BLOCK, width), jnp.bfloat16),
        compiler_params=pltpu.CompilerParams(vmem_limit_bytes=8 << 20),
        name="total",
    )(*parts)


def serve_body(table, u0, u1, u2, v0, v1, v2):
    chunk = pl.program_id(0)
    ins, outs = (u0, u1, u2), (v0, v1, v2)
    for place in range(16):
        for k in range(3):
            entry = k * 256 + chunk * 32 + place * 2
            for rank in range(2):
                half = jnp.minimum(table[entry + rank], HALVES - 1)
                outs[k][0, place * 2 + rank] = ins[k][place, half]


def serve(table, parts):
    width = parts[0].shape[-1]
    return pl.pallas_call(
        serve_body,
        grid_spec=pltpu.PrefetchScalarGridSpec(
            num_scalar_prefetch=1,
            grid=(8,),
            in_specs=[
                pl.BlockSpec((16, HALVES, n, width), lambda i, t: (0, 0, 0, 0))
                for _, n in PARTS
            ],
            out_specs=[pl.BlockSpec((1, 32, n, width), lambda i, t: (i, 0, 0, 0)) for _, n in PARTS],
        ),
        out_shape=[jax.ShapeDtypeStruct((8, 32, n, width), jnp.bfloat16) for _, n in PARTS],
        compiler_params=pltpu.CompilerParams(vmem_limit_bytes=16 << 20),
        name="serve",
    )(table, *parts)


def pull_body(table, blocks, pre_conv, w0, w1, w2, out, sums):
    ins = (w0, w1, w2)
    sums[...] = jnp.zeros_like(sums)

    def some(step, carry):
        for b in range(GROUP):
            block = step * GROUP + b
            grad = jnp.concatenate([ins[k][table[1 + k, block]] for k in range(3)], axis=0)
            sums[table[0, block]] += jnp.dot(
                grad, blocks[block], preferred_element_type=jnp.float32
            )
        return carry

    lax.fori_loop(0, blocks.shape[0] // GROUP, some, 0)
    for k in range(sums.shape[0]):
        cells = slice(k * BLOCK, (k + 1) * BLOCK)
        out[:, cells] = (sums[k] * silu_slope(pre_conv[:, cells])).astype(out.dtype)


def pull(table, regrid_blocks, pre_conv, parts):
    cells, width = regrid_blocks.shape[2], pre_conv.shape[0]
    vmem = pl.BlockSpec(memory_space=pltpu.VMEM)
    return pl.pallas_call(
        pull_body,
        in_specs=[pl.BlockSpec(memory_space=pltpu.SMEM)] + [vmem] * 5,
        out_specs=vmem,
        scratch_shapes=[pltpu.VMEM((pre_conv.shape[1] // BLOCK, width, cells), jnp.float32)],
        out_shape=jax.ShapeDtypeStruct(pre_conv.shape, jnp.bfloat16),
        compiler_params=pltpu.CompilerParams(vmem_limit_bytes=24 << 20),
        name="pull",
    )(table, regrid_blocks, pre_conv, *[part.reshape(256, *part.shape[2:]) for part in parts])


def tiles_body(beside, latent, weights, scale, codes, grad, edges, rims0, rims1, near_grad, sends, recvs):
    lon, lat = lax.axis_index("lon"), lax.axis_index("lat")
    lons, lats = lax.axis_size("lon"), lax.axis_size("lat")
    above, below = (lon + 1) % lons, (lon + lons - 1) % lons
    barrier = pltpu.get_barrier_semaphore()
    peers = []
    for step in range(lats):
        row = (lat + step) % lats
        peers += [(above, row), (below, row)] + ([(lon, row)] if step else [])
    for peer in peers:
        pl.semaphore_signal(barrier, inc=1, device_id=peer, device_id_type=MESH)

    pixels = TS * TS
    tiles = latent.shape[0] // pixels
    rims = (rims0, rims1)

    def iota(shape, dim):
        return lax.broadcasted_iota(jnp.int32, shape, dim)

    edge, cell = iota((4 * TS, pixels), 0), iota((4 * TS, pixels), 1)
    side, spot = edge >> 4, edge & 15
    wanted = jnp.where(
        side == 0,
        spot,
        jnp.where(side == 1, TS * spot + TS - 1, jnp.where(side == 2, pixels - TS + spot, TS * spot)),
    )
    take_edges = (cell == wanted).astype(jnp.float32).astype(jnp.bfloat16)
    one, other = iota((pixels, pixels), 0), iota((pixels, pixels), 1)
    apart = jnp.abs((one >> 4) - (other >> 4)) + jnp.abs((one & 15) - (other & 15))
    adjacent = (apart == 1).astype(jnp.float32).astype(jnp.bfloat16)
    cell, edge = iota((pixels, 4 * TS), 0), iota((pixels, 4 * TS), 1)
    side, spot = edge >> 4, edge & 15
    row, column = cell >> 4, cell & 15
    along = jnp.where((side & 1) == 0, column, row)
    inward = jnp.where(
        side == 0,
        row,
        jnp.where(side == 1, TS - 1 - column, jnp.where(side == 2, TS - 1 - row, column)),
    )

    def dot(a, b):
        return jnp.dot(a, b, preferred_element_type=jnp.float32)

    def dot_turned(a, b):
        return lax.dot_general(a, b, (((1,), (1,)), ((), ())), preferred_element_type=jnp.float32)

    def swap(turn, values):
        for t in range(tiles):
            picked = dot(take_edges, values[t * pixels : (t + 1) * pixels, :]).astype(jnp.bfloat16)
            for s in range(4):
                edges[turn, s, t] = picked[s * TS : (s + 1) * TS]
        mine = pl.ds(lat * tiles, tiles)
        copies = []
        for step in range(lats):
            row = (lat + step) % lats
            ways = [(2, 0, below), (0, 2, above)] + ([(1, 3, lon), (3, 1, lon)] if step else [])
            for from_side, to_side, column in ways:
                copy = pltpu.make_async_remote_copy(
                    src_ref=edges.at[turn, from_side],
                    dst_ref=rims[turn].at[to_side, mine],
                    send_sem=sends.at[turn, to_side, step],
                    recv_sem=recvs.at[turn, to_side, step],
                    device_id=(column, row),
                    device_id_type=MESH,
                )
                copy.start()
                copies.append(copy)
        rims[turn][3, mine] = edges[turn, 1]
        rims[turn][1, mine] = edges[turn, 3]
        return copies

    def around(turn, t, values):
        flips = jnp.zeros_like(edge)
        found = []
        for s in range(4):
            flips = jnp.where(side == s, beside[t * 8 + s * 2 + 1], flips)
            found.append(rims[turn][s, beside[t * 8 + s * 2]])
        hit = (inward == 0) & (spot == jnp.where(flips == 1, TS - 1 - along, along))
        place = hit.astype(jnp.float32).astype(jnp.bfloat16)
        return dot(adjacent, values[t * pixels : (t + 1) * pixels, :]) + dot(
            place, jnp.concatenate(found, axis=0)
        )

    pl.semaphore_wait(barrier, len(peers))
    copies = swap(0, latent)
    for copy in copies:
        copy.wait()
    mix_grads = []
    for t in range(tiles):
        cells = slice(t * pixels, (t + 1) * pixels)
        near_sum = around(0, t, latent).astype(jnp.bfloat16)
        pre_mix = dot(latent[cells, :], weights[0]) + dot(near_sum, weights[1])
        mixed = pre_mix * jax.nn.sigmoid(pre_mix)
        codes[cells, :] = mixed.astype(jnp.bfloat16)
        mix_grad = (laplace_slope(mixed, scale[...]) * silu_slope(pre_mix)).astype(jnp.bfloat16)
        near_grad[cells, :] = dot_turned(mix_grad, weights[1]).astype(jnp.bfloat16)
        mix_grads.append(mix_grad)
    copies = swap(1, near_grad)
    own = [dot_turned(mix_grad, weights[0]) for mix_grad in mix_grads]
    for copy in copies:
        copy.wait()
    for t in range(tiles):
        found = own[t] + around(1, t, near_grad)
        for h in range(pixels // BLOCK):
            part = found[h * BLOCK : (h + 1) * BLOCK, :]
            grad[t * (pixels // BLOCK) + h] = part.T.astype(jnp.bfloat16)


def tile_stage(latent, neighbours, hp_weight, rate_scale, collective_id):
    tiles, width = neighbours.shape[0], latent.shape[1]
    column_tiles = tiles * lax.axis_size("lat")
    beside = jnp.stack([neighbours[:, :, 0] % column_tiles, neighbours[:, :, 2]], axis=-1)
    vmem = pl.BlockSpec(memory_space=pltpu.VMEM)
    return pl.pallas_call(
        tiles_body,
        out_shape=[
            jax.ShapeDtypeStruct(latent.shape, jnp.bfloat16),
            jax.ShapeDtypeStruct((latent.shape[0] // BLOCK, width, BLOCK), jnp.bfloat16),
        ],
        in_specs=[pl.BlockSpec(memory_space=pltpu.SMEM), vmem, vmem, vmem],
        out_specs=[vmem, vmem],
        scratch_shapes=[
            pltpu.VMEM((2, 4, tiles, TS, width), jnp.bfloat16),
            pltpu.VMEM((4, column_tiles, TS, width), jnp.bfloat16),
            pltpu.VMEM((4, column_tiles, TS, width), jnp.bfloat16),
            pltpu.VMEM(latent.shape, jnp.bfloat16),
            pltpu.SemaphoreType.DMA((2, 4, 4)),
            pltpu.SemaphoreType.DMA((2, 4, 4)),
        ],
        compiler_params=pltpu.CompilerParams(collective_id=collective_id, has_side_effects=True, vmem_limit_bytes=4 << 20),
        name="tile_stage",
    )(beside.reshape(-1), latent, hp_weight, rate_scale.reshape(1, width))


def routing(source_block, target_device, target_half):
    here = torus_position()
    count = source_block.shape[0]

    def rows_of(values):
        grid = values.reshape(4, 4, 2, 4, count)
        picks = []
        for k in range(3):
            start = [here["z"], here["x"], 0, here["y"], 0]
            size = [1, 1, 2, 1, count]
            at = {"z": 0, "x": 1, "y": 3}[LINE[k]]
            start[at], size[at] = 0, 4
            picks.append(lax.dynamic_slice(grid, start, size).reshape(8, count))
        own = lax.dynamic_slice(
            grid, [here["z"], here["x"], here["c"], here["y"], 0], [1, 1, 1, 1, count]
        )
        return jnp.concatenate(picks + [own.reshape(1, count)], axis=0)

    targets = rows_of(target_device[:, 0])
    halves = rows_of(target_half)[:24]
    ids = jnp.arange(count, dtype=jnp.int32)
    rank = jnp.sum(
        (targets[:, :, None] == targets[:, None, :]) & (ids[None, None, :] < ids[None, :, None]),
        axis=2,
        dtype=jnp.int32,
    )
    to = {"z": targets // 32, "x": (targets // 8) % 4, "c": (targets // 4) % 2, "y": targets % 4}
    codes, order = [], []
    for k in range(3):
        rows = slice(8 * k, 8 * k + 8)
        fits = (to["c"][rows] == here["c"]) & (to[LINE[k]][rows] == here[LINE[k]])
        first, second = [
            (to[axis][rows] - here[axis] + RING) % RING for axis in PLANE[k]
        ]
        codes.append(jnp.where(fits, (first * RING + second) * 2 + rank[rows], -1))
        index = jnp.arange(8, dtype=jnp.int32)
        line, core = (index % RING, index // RING) if k == 0 else (index // 2, index % 2)
        order.append((here[LINE[k]] - line + RING) % RING * 2 + (core + here["c"]) % 2)
    codes = jnp.concatenate(codes, axis=0)
    slots = jnp.arange(32, dtype=jnp.int32)
    found = jnp.sum(
        jnp.where(codes[:, None, :] == slots[None, :, None], (halves - HALVES)[:, None, :], 0),
        axis=2,
    )
    chunk = jnp.arange(8, dtype=jnp.int32)
    table = HALVES + jnp.sum(
        jnp.where(
            jnp.stack(order)[:, None, :, None] == chunk[None, :, None, None],
            found.reshape(3, 1, 8, 32),
            0,
        ),
        axis=2,
    )
    own = {axis: value[24] for axis, value in to.items()}
    away = {axis: (own[axis] - here[axis] + RING) % RING for axis in ("z", "x", "y")}
    flip = (own["c"] + here["c"]) % 2
    lines = [source_block]
    for k in range(3):
        place = away[PLANE[k][0]] * RING + away[PLANE[k][1]]
        lines.append((away[LINE[k]] * 2 + flip) * 32 + place * 2 + rank[24])
    return table.reshape(-1), jnp.stack(lines)


def on_device(
    fields,
    conv_weight,
    regrid_blocks,
    source_block,
    target_device,
    target_half,
    neighbours,
    hp_weight,
    rate_scale,
):
    channels, lon_cells, lat_cells = fields.shape
    latent_width = conv_weight.shape[1]
    table, lines = routing(source_block, target_device, target_half)
    pre_conv = conv_taps(conv_weight, grid_rims(fields), False)
    hidden = jax.nn.silu(pre_conv).astype(jnp.bfloat16)
    outgoing = spread(lines, hidden, regrid_blocks)
    arrived = line_exchange(outgoing, 1, 0)
    partial = combine(table, arrived)
    latent_in = total(plane_scatter(partial, 1))
    codes, halves_grad = tile_stage(
        latent_in.reshape(-1, latent_width), neighbours, hp_weight, rate_scale, 4
    )
    replies = serve(table, plane_gather(halves_grad, 2))
    answers = line_exchange(replies, -1, 3)
    pre_grad = pull(lines, regrid_blocks, pre_conv, answers).reshape(
        latent_width, lon_cells, lat_cells
    )
    grad_fields = conv_taps(conv_weight, grid_rims(pre_grad), True).reshape(
        channels, lon_cells, lat_cells
    )
    return (codes, grad_fields)


def solution(mesh):
    placed = (
        P(None, "lon", "lat"),
        P(),
        P(("lon", "lat"), None, None),
        P(("lon", "lat")),
        P(),
        P(),
        P(("lon", "lat"), None, None),
        P(),
        P(),
    )
    return jax.shard_map(
        on_device,
        mesh=mesh,
        in_specs=placed,
        out_specs=(P(("lon", "lat"), None), P(None, "lon", "lat")),
        check_vma=False,
    )
```

```python
import functools

import jax
import jax.numpy as jnp
from jax import lax
from jax.experimental import pallas as pl
from jax.experimental.pallas import tpu as pltpu
from jax.sharding import PartitionSpec as P

TS = 16
RING = 4
BLOCK = 128
HALVES = 8
GROUP = 8
MESH = pl.DeviceIdType.MESH
LOG_TWO = 0.6931471805599453

PARTS = ((0, 48), (48, 48), (96, 32))
LINE = ("y", "z", "x")
PLANE = (("z", "x"), ("x", "y"), ("y", "z"))


def extended(cells, sides, width):
    for axis, dim in sides:
        count = lax.axis_size(axis)
        head = lax.slice_in_dim(cells, 0, width, axis=dim)
        tail = lax.slice_in_dim(cells, cells.shape[dim] - width, cells.shape[dim], axis=dim)
        cells = jnp.concatenate(
            [
                lax.ppermute(tail, axis, [(i, (i + 1) % count) for i in range(count)]),
                cells,
                lax.ppermute(head, axis, [((i + 1) % count, i) for i in range(count)]),
            ],
            axis=dim,
        )
    return cells


def silu_slope(values):
    sigma = jax.nn.sigmoid(values)
    return sigma * (1.0 + values * (1.0 - sigma))


def laplace_slope(latent, spread):
    inverse = 1.0 / spread
    half_mass = 0.5 * jnp.exp(-0.5 * inverse)
    far = inverse * (1.0 / LOG_TWO)
    scaled = jnp.clip(latent, -0.5, 0.5) * inverse
    grown, shrunk = jnp.exp(scaled), jnp.exp(-scaled)
    slope_near = (half_mass * far) * (grown - shrunk) / (1.0 - half_mass * (grown + shrunk))
    slope_far = jnp.where(latent > 0.0, far, -far)
    return jnp.where(jnp.abs(latent) < 0.5, slope_near, slope_far)


def conv_taps(kernel, padded, reverse):
    lon_cells = padded.shape[1] - 2
    lat_cells = padded.shape[2] - 2
    out_rows = kernel.shape[2] if reverse else kernel.shape[1]
    result = jnp.zeros((out_rows, lon_cells * lat_cells), jnp.float32)
    for tap_index in range(9):
        lon_shift = tap_index // 3
        lat_shift = tap_index % 3
        if reverse:
            lon_shift = 2 - lon_shift
            lat_shift = 2 - lat_shift
        window = padded[
            :, lon_shift : lon_shift + lon_cells, lat_shift : lat_shift + lat_cells
        ].reshape(padded.shape[0], lon_cells * lat_cells)
        if reverse:
            result = result + lax.dot_general(
                kernel[tap_index],
                window,
                (((0,), (0,)), ((), ())),
                preferred_element_type=jnp.float32,
            )
        else:
            result = result + jnp.dot(kernel[tap_index], window, preferred_element_type=jnp.float32)
    return result


def grid_rims(values):
    padded = extended(values, (("lon", 1), ("lat", 2)), 1)
    lat_pos = lax.axis_index("lat")
    lat_last = lax.axis_size("lat") - 1
    column = lax.broadcasted_iota(jnp.int32, (1, 1, padded.shape[2]), 2)
    outside = (column == 0) & (lat_pos == 0) | (column == padded.shape[2] - 1) & (
        lat_pos == lat_last
    )
    return jnp.where(outside, jnp.zeros_like(padded), padded)


def torus_position():
    lon = lax.axis_index("lon")
    return {"z": lon // 8, "x": (lon // 2) % 4, "c": lon % 2, "y": lax.axis_index("lat")}


def moved(here, **steps):
    place = dict(here)
    for axis, step in steps.items():
        if axis == "c":
            place["c"] = (here["c"] + step) % 2
        else:
            place[axis] = (here[axis] + step + RING) % RING
    return place


def device_at(place):
    return (place["z"] * 8 + place["x"] * 2 + place["c"], place["y"])


def meet(peers):
    barrier = pltpu.get_barrier_semaphore()
    for peer in peers:
        pl.semaphore_signal(barrier, inc=1, device_id=device_at(peer), device_id_type=MESH)
    pl.semaphore_wait(barrier, len(peers))


def line_body(sign, s0, s1, s2, r0, r1, r2, send, recv, local):
    here = torus_position()
    peers = [moved(here, c=1)]
    for axis in LINE:
        for step in range(1, RING):
            for flip in range(2):
                peers.append(moved(here, **{axis: step, "c": flip}))
    meet(peers)
    sources, targets = (s0, s1, s2), (r0, r1, r2)
    copies = []
    for chunk in (4, 5, 2, 3, 6, 7, 1):
        step, flip = chunk // 2, chunk % 2
        for k in range(3):
            copy = pltpu.make_async_remote_copy(
                src_ref=sources[k].at[chunk],
                dst_ref=targets[k].at[chunk],
                send_sem=send.at[k, chunk],
                recv_sem=recv.at[k, chunk],
                device_id=device_at(moved(here, **{LINE[k]: sign * step, "c": flip})),
                device_id_type=MESH,
            )
            copy.start()
            copies.append(copy)
    own = []
    for k in range(3):
        copy = pltpu.make_async_copy(sources[k].at[0], targets[k].at[0], local.at[k])
        copy.start()
        own.append(copy)
    for copy in own + copies:
        copy.wait()


def line_exchange(parts, sign, collective_id):
    anywhere = pl.BlockSpec(memory_space=pl.ANY)
    return pl.pallas_call(
        functools.partial(line_body, sign),
        out_shape=[jax.ShapeDtypeStruct(part.shape, part.dtype) for part in parts],
        in_specs=[anywhere] * 3,
        out_specs=[anywhere] * 3,
        scratch_shapes=[
            pltpu.SemaphoreType.DMA((3, 8)),
            pltpu.SemaphoreType.DMA((3, 8)),
            pltpu.SemaphoreType.DMA((3,)),
        ],
        compiler_params=pltpu.CompilerParams(collective_id=collective_id, has_side_effects=True, vmem_limit_bytes=4 << 20),
        name="line_exchange_%d" % collective_id,
    )(*parts)


def spread_body(table, hidden, blocks, o0, o1, o2, turned):
    outs = (o0, o1, o2)
    for k in range(turned.shape[0]):
        turned[k] = hidden[:, k * BLOCK : (k + 1) * BLOCK].T

    def some(step, carry):
        for b in range(GROUP):
            block = step * GROUP + b
            made = jnp.dot(
                blocks[block], turned[table[0, block]], preferred_element_type=jnp.float32
            ).astype(jnp.bfloat16)
            for k, (start, count) in enumerate(PARTS):
                outs[k][table[1 + k, block]] = made[start : start + count]
        return carry

    lax.fori_loop(0, blocks.shape[0] // GROUP, some, 0)


def spread(table, hidden, regrid_blocks):
    cells, width = regrid_blocks.shape[2], hidden.shape[0]
    vmem = pl.BlockSpec(memory_space=pltpu.VMEM)
    parts = pl.pallas_call(
        spread_body,
        in_specs=[pl.BlockSpec(memory_space=pltpu.SMEM), vmem, vmem],
        out_specs=[vmem] * 3,
        scratch_shapes=[pltpu.VMEM((hidden.shape[1] // BLOCK, cells, width), jnp.bfloat16)],
        out_shape=[jax.ShapeDtypeStruct((256, n, width), jnp.bfloat16) for _, n in PARTS],
        compiler_params=pltpu.CompilerParams(vmem_limit_bytes=24 << 20),
        name="spread",
    )(table, hidden, regrid_blocks)
    return [part.reshape(8, 32, *part.shape[1:]) for part in parts]


def combine_body(table, r0, r1, r2, p0, p1, p2, a0, a1, a2):
    place = pl.program_id(0)
    ins, outs, sums = (r0, r1, r2), (p0, p1, p2), (a0, a1, a2)
    for total in sums:
        total[...] = jnp.zeros_like(total)
    for chunk in range(8):
        for k in range(3):
            entry = k * 256 + chunk * 32 + place * 2
            for rank in range(2):
                half = table[entry + rank]
                sums[k][half] += ins[k][chunk, rank].astype(jnp.float32)
    for k in range(3):
        outs[k][0] = sums[k][:HALVES].astype(jnp.bfloat16)


def combine(table, parts):
    width = parts[0].shape[-1]
    return pl.pallas_call(
        combine_body,
        grid_spec=pltpu.PrefetchScalarGridSpec(
            num_scalar_prefetch=1,
            grid=(16,),
            in_specs=[pl.BlockSpec((8, 2, n, width), lambda i, t: (0, i, 0, 0)) for _, n in PARTS],
            out_specs=[
                pl.BlockSpec((1, HALVES, n, width), lambda i, t: (i, 0, 0, 0)) for _, n in PARTS
            ],
            scratch_shapes=[pltpu.VMEM((HALVES + 1, n, width), jnp.float32) for _, n in PARTS],
        ),
        out_shape=[jax.ShapeDtypeStruct((16, HALVES, n, width), jnp.bfloat16) for _, n in PARTS],
        compiler_params=pltpu.CompilerParams(vmem_limit_bytes=8 << 20),
        name="combine",
    )(table, *parts)


def pull_body(table, blocks, pre_conv, w0, w1, w2, out, sums):
    ins = (w0, w1, w2)
    sums[...] = jnp.zeros_like(sums)

    def some(step, carry):
        for b in range(GROUP):
            block = step * GROUP + b
            grad = jnp.concatenate([ins[k][table[1 + k, block]] for k in range(3)], axis=0)
            sums[table[0, block]] += jnp.dot(
                grad, blocks[block], preferred_element_type=jnp.float32
            )
        return carry

    lax.fori_loop(0, blocks.shape[0] // GROUP, some, 0)
    for k in range(sums.shape[0]):
        cells = slice(k * BLOCK, (k + 1) * BLOCK)
        out[:, cells] = (sums[k] * silu_slope(pre_conv[:, cells])).astype(out.dtype)


def pull(table, regrid_blocks, pre_conv, parts):
    cells, width = regrid_blocks.shape[2], pre_conv.shape[0]
    vmem = pl.BlockSpec(memory_space=pltpu.VMEM)
    return pl.pallas_call(
        pull_body,
        in_specs=[pl.BlockSpec(memory_space=pltpu.SMEM)] + [vmem] * 5,
        out_specs=vmem,
        scratch_shapes=[pltpu.VMEM((pre_conv.shape[1] // BLOCK, width, cells), jnp.float32)],
        out_shape=jax.ShapeDtypeStruct(pre_conv.shape, jnp.bfloat16),
        compiler_params=pltpu.CompilerParams(vmem_limit_bytes=24 << 20),
        name="pull",
    )(table, regrid_blocks, pre_conv, *[part.reshape(256, *part.shape[2:]) for part in parts])


def remote(source, target, send, recv, place):
    copy = pltpu.make_async_remote_copy(
        src_ref=source,
        dst_ref=target,
        send_sem=send,
        recv_sem=recv,
        device_id=place,
        device_id_type=MESH,
    )
    copy.start()
    return copy


def iota(shape, dim):
    return lax.broadcasted_iota(jnp.int32, shape, dim)


def dot(a, b):
    return jnp.dot(a, b, preferred_element_type=jnp.float32)


def dot_turned(a, b):
    return lax.dot_general(a, b, (((1,), (1,)), ((), ())), preferred_element_type=jnp.float32)


def edge_masks(pixels):
    edge, cell = iota((4 * TS, pixels), 0), iota((4 * TS, pixels), 1)
    side, spot = edge >> 4, edge & 15
    wanted = jnp.where(
        side == 0,
        spot,
        jnp.where(side == 1, TS * spot + TS - 1, jnp.where(side == 2, pixels - TS + spot, TS * spot)),
    )
    take_edges = (cell == wanted).astype(jnp.float32).astype(jnp.bfloat16)
    one, other = iota((pixels, pixels), 0), iota((pixels, pixels), 1)
    apart = jnp.abs((one >> 4) - (other >> 4)) + jnp.abs((one & 15) - (other & 15))
    adjacent = (apart == 1).astype(jnp.float32).astype(jnp.bfloat16)
    cell, edge = iota((pixels, 4 * TS), 0), iota((pixels, 4 * TS), 1)
    side, spot = edge >> 4, edge & 15
    row, column = cell >> 4, cell & 15
    along = jnp.where((side & 1) == 0, column, row)
    inward = jnp.where(
        side == 0,
        row,
        jnp.where(side == 1, TS - 1 - column, jnp.where(side == 2, TS - 1 - row, column)),
    )
    return take_edges, adjacent, side, spot, along, inward


def middle_body(
    table, beside, p0, p1, p2, weights, scale, codes, w0, w1, w2,
    a0, a1, a2, b0, b1, b2, c0, c1, c2, latent, grad, edges, rims0, rims1, near_grad,
    u0, u1, u2, v0, v1, v2, first_sems, second_sems, edge_sems, gather_sems, line_sems,
):
    ps, ws, arrived, sums, landed = (p0, p1, p2), (w0, w1, w2), (a0, a1, a2), (b0, b1, b2), (c0, c1, c2)
    us, vs, rims = (u0, u1, u2), (v0, v1, v2), (rims0, rims1)
    here = torus_position()
    lon, lat = lax.axis_index("lon"), lax.axis_index("lat")
    lons, lats = lax.axis_size("lon"), lax.axis_size("lat")
    above, below = (lon + 1) % lons, (lon + lons - 1) % lons
    pixels = TS * TS
    per_tile = pixels // BLOCK
    tiles = latent.shape[0] // per_tile
    columns = [(k, start, count) for k, (start, count) in enumerate(PARTS)]

    barrier = pltpu.get_barrier_semaphore()
    peers = [device_at(moved(here, c=1))]
    for axis in LINE:
        for step in range(1, RING):
            for flip in range(2):
                peers.append(device_at(moved(here, **{axis: step, "c": flip})))
    for step in range(lats):
        row = (lat + step) % lats
        peers += [(above, row), (below, row)]
    for peer in peers:
        pl.semaphore_signal(barrier, inc=1, device_id=peer, device_id_type=MESH)
    pl.semaphore_wait(barrier, len(peers))

    copies = {}
    for step in (2, 1, 3):
        for k in range(3):
            copies[k, step] = remote(
                ps[k].at[:, step],
                arrived[k].at[step],
                first_sems.at[0, k, step],
                first_sems.at[1, k, step],
                device_at(moved(here, **{PLANE[k][1]: step})),
            )
    take_edges, adjacent, side, spot, along, inward = edge_masks(pixels)
    for copy in copies.values():
        copy.wait()
    copies = []
    for step in (2, 1, 3, 0):
        for k in range(3):
            total = ps[k][step, 0].astype(jnp.float32)
            for other in range(1, RING):
                total += arrived[k][other, step].astype(jnp.float32)
            sums[k][step] = total.astype(jnp.bfloat16)
            if step:
                copies.append(
                    remote(
                        sums[k].at[step],
                        landed[k].at[step],
                        second_sems.at[0, k, step],
                        second_sems.at[1, k, step],
                        device_at(moved(here, **{PLANE[k][0]: step})),
                    )
                )
    for copy in copies:
        copy.wait()
    for k, start, count in columns:
        total = sums[k][0].astype(jnp.float32)
        for step in range(1, RING):
            total += landed[k][step].astype(jnp.float32)
        latent[:, start : start + count] = total.astype(jnp.bfloat16)

    def tile_of(values, t):
        return values[t * per_tile : (t + 1) * per_tile].reshape(pixels, values.shape[2])

    def swap(turn, values):
        for t in range(tiles):
            picked = dot(take_edges, tile_of(values, t)).astype(jnp.bfloat16)
            for s in range(4):
                edges[turn, s, t] = picked[s * TS : (s + 1) * TS]
        mine = pl.ds(lat * tiles, tiles)
        sent = []
        for step in (2, 1, 3, 0):
            row = (lat + step) % lats
            ways = [(2, 0, below), (0, 2, above)] + ([(1, 3, lon), (3, 1, lon)] if step else [])
            for from_side, to_side, column in ways:
                sent.append(
                    remote(
                        edges.at[turn, from_side],
                        rims[turn].at[to_side, mine],
                        edge_sems.at[0, turn, to_side, step],
                        edge_sems.at[1, turn, to_side, step],
                        (column, row),
                    )
                )
        rims[turn][3, mine] = edges[turn, 1]
        rims[turn][1, mine] = edges[turn, 3]
        return sent

    def placed(t):
        flips = jnp.zeros_like(side)
        for s in range(4):
            flips = jnp.where(side == s, beside[t * 8 + s * 2 + 1], flips)
        hit = (inward == 0) & (spot == jnp.where(flips == 1, TS - 1 - along, along))
        return hit.astype(jnp.float32).astype(jnp.bfloat16)

    def outer(turn, t, place):
        found = [rims[turn][s, beside[t * 8 + s * 2]] for s in range(4)]
        return dot(place, jnp.concatenate(found, axis=0))

    copies = swap(0, latent)
    places = [placed(t) for t in range(tiles)]
    inner = [dot(adjacent, tile_of(latent, t)) for t in range(tiles)]
    mixes = [dot(tile_of(latent, t), weights[0]) for t in range(tiles)]
    for copy in copies:
        copy.wait()
    mix_grads = []
    for t in range(tiles):
        near_sum = (inner[t] + outer(0, t, places[t])).astype(jnp.bfloat16)
        pre_mix = mixes[t] + dot(near_sum, weights[1])
        mixed = pre_mix * jax.nn.sigmoid(pre_mix)
        codes[t * pixels : (t + 1) * pixels, :] = mixed.astype(jnp.bfloat16)
        mix_grad = (laplace_slope(mixed, scale[...]) * silu_slope(pre_mix)).astype(jnp.bfloat16)
        made = dot_turned(mix_grad, weights[1]).astype(jnp.bfloat16)
        near_grad[t * per_tile : (t + 1) * per_tile] = made.reshape(per_tile, BLOCK, -1)
        mix_grads.append(mix_grad)
    copies = swap(1, near_grad)
    own = [
        dot_turned(mix_grads[t], weights[0]) + dot(adjacent, tile_of(near_grad, t))
        for t in range(tiles)
    ]
    for copy in copies:
        copy.wait()
    for t in range(tiles):
        found = own[t] + outer(1, t, places[t])
        for h in range(per_tile):
            part = found[h * BLOCK : (h + 1) * BLOCK, :]
            grad[t * per_tile + h] = part.T.astype(jnp.bfloat16)

    def gathered(k, source, place, axis, step):
        return remote(
            source,
            us[k].at[place],
            gather_sems.at[0, k, place],
            gather_sems.at[1, k, place],
            device_at(moved(here, **{axis: -step})),
        )

    first, later = {}, []
    mine = [grad.at[:, pl.ds(start, count)] for start, count in PARTS]
    for step in (2, 1, 3):
        for k in range(3):
            first[k, step] = gathered(k, mine[k], step, PLANE[k][1], step)
    for step in (2, 1, 3):
        for k in range(3):
            later.append(gathered(k, mine[k], step * RING, PLANE[k][0], step))
    for k, start, count in columns:
        us[k][0] = grad[:, start : start + count]
    for step in (1, 3, 2):
        for k in range(3):
            first[k, step].wait_recv()
            for hop in (2, 1, 3):
                later.append(gathered(k, us[k].at[step], hop * RING + step, PLANE[k][0], hop))
    for copy in later:
        copy.wait()
    for copy in first.values():
        copy.wait_send()

    copies = []
    for chunk in (4, 5, 2, 3, 6, 7, 1, 0):
        step, flip = chunk // 2, chunk % 2

        def fill(place, carry):
            for k in range(3):
                for rank in range(2):
                    half = jnp.minimum(table[k * 256 + chunk * 32 + place * 2 + rank], HALVES - 1)
                    found = us[k][place, half]
                    if chunk:
                        vs[k][chunk - 1, place * 2 + rank] = found
                    else:
                        ws[k][0, place * 2 + rank] = found
            return carry

        lax.fori_loop(0, RING * RING, fill, 0)
        if chunk:
            for k in range(3):
                copies.append(
                    remote(
                        vs[k].at[chunk - 1],
                        ws[k].at[chunk],
                        line_sems.at[0, k, chunk],
                        line_sems.at[1, k, chunk],
                        device_at(moved(here, **{LINE[k]: -step, "c": flip})),
                    )
                )
    for copy in copies:
        copy.wait()


def middle(table, neighbours, parts, hp_weight, rate_scale, collective_id):
    tiles, width = neighbours.shape[0], hp_weight.shape[1]
    column_tiles = tiles * lax.axis_size("lat")
    pixels = tiles * TS * TS
    beside = jnp.stack([neighbours[:, :, 0] % column_tiles, neighbours[:, :, 2]], axis=-1)
    smem, vmem = pl.BlockSpec(memory_space=pltpu.SMEM), pl.BlockSpec(memory_space=pltpu.VMEM)
    counts = [count for _, count in PARTS]

    def buffers(*lead):
        return [pltpu.VMEM((*lead, n, width), jnp.bfloat16) for n in counts]

    return pl.pallas_call(
        middle_body,
        out_shape=[jax.ShapeDtypeStruct((pixels, width), jnp.bfloat16)]
        + [jax.ShapeDtypeStruct((8, 32, n, width), jnp.bfloat16) for n in counts],
        in_specs=[smem, smem] + [vmem] * 5,
        out_specs=[vmem] * 4,
        scratch_shapes=buffers(RING, RING, HALVES)
        + buffers(RING, HALVES)
        + buffers(RING, HALVES)
        + [
            pltpu.VMEM((HALVES, BLOCK, width), jnp.bfloat16),
            pltpu.VMEM((HALVES, width, BLOCK), jnp.bfloat16),
            pltpu.VMEM((2, 4, tiles, TS, width), jnp.bfloat16),
            pltpu.VMEM((4, column_tiles, TS, width), jnp.bfloat16),
            pltpu.VMEM((4, column_tiles, TS, width), jnp.bfloat16),
            pltpu.VMEM((HALVES, BLOCK, width), jnp.bfloat16),
        ]
        + buffers(RING * RING, HALVES)
        + buffers(7, 32)
        + [
            pltpu.SemaphoreType.DMA((2, 3, RING)),
            pltpu.SemaphoreType.DMA((2, 3, RING)),
            pltpu.SemaphoreType.DMA((2, 2, 4, 4)),
            pltpu.SemaphoreType.DMA((2, 3, RING * RING)),
            pltpu.SemaphoreType.DMA((2, 3, 8)),
        ],
        compiler_params=pltpu.CompilerParams(
            collective_id=collective_id, has_side_effects=True, vmem_limit_bytes=36 << 20
        ),
        name="middle",
    )(
        table,
        beside.reshape(-1),
        *[part.reshape(RING, RING, *part.shape[1:]) for part in parts],
        hp_weight,
        rate_scale.reshape(1, width),
    )


def routing(source_block, target_device, target_half):
    here = torus_position()
    count = source_block.shape[0]

    def rows_of(values):
        grid = values.reshape(4, 4, 2, 4, count)
        picks = []
        for k in range(3):
            start = [here["z"], here["x"], 0, here["y"], 0]
            size = [1, 1, 2, 1, count]
            at = {"z": 0, "x": 1, "y": 3}[LINE[k]]
            start[at], size[at] = 0, 4
            picks.append(lax.dynamic_slice(grid, start, size).reshape(8, count))
        own = lax.dynamic_slice(
            grid, [here["z"], here["x"], here["c"], here["y"], 0], [1, 1, 1, 1, count]
        )
        return jnp.concatenate(picks + [own.reshape(1, count)], axis=0)

    targets = rows_of(target_device[:, 0])
    halves = rows_of(target_half)[:24]
    ids = jnp.arange(count, dtype=jnp.int32)
    rank = jnp.sum(
        (targets[:, :, None] == targets[:, None, :]) & (ids[None, None, :] < ids[None, :, None]),
        axis=2,
        dtype=jnp.int32,
    )
    to = {"z": targets // 32, "x": (targets // 8) % 4, "c": (targets // 4) % 2, "y": targets % 4}
    codes, order = [], []
    for k in range(3):
        rows = slice(8 * k, 8 * k + 8)
        fits = (to["c"][rows] == here["c"]) & (to[LINE[k]][rows] == here[LINE[k]])
        first, second = [
            (to[axis][rows] - here[axis] + RING) % RING for axis in PLANE[k]
        ]
        codes.append(jnp.where(fits, (first * RING + second) * 2 + rank[rows], -1))
        index = jnp.arange(8, dtype=jnp.int32)
        line, core = (index % RING, index // RING) if k == 0 else (index // 2, index % 2)
        order.append((here[LINE[k]] - line + RING) % RING * 2 + (core + here["c"]) % 2)
    codes = jnp.concatenate(codes, axis=0)
    slots = jnp.arange(32, dtype=jnp.int32)
    found = jnp.sum(
        jnp.where(codes[:, None, :] == slots[None, :, None], (halves - HALVES)[:, None, :], 0),
        axis=2,
    )
    chunk = jnp.arange(8, dtype=jnp.int32)
    table = HALVES + jnp.sum(
        jnp.where(
            jnp.stack(order)[:, None, :, None] == chunk[None, :, None, None],
            found.reshape(3, 1, 8, 32),
            0,
        ),
        axis=2,
    )
    own = {axis: value[24] for axis, value in to.items()}
    away = {axis: (own[axis] - here[axis] + RING) % RING for axis in ("z", "x", "y")}
    flip = (own["c"] + here["c"]) % 2
    lines = [source_block]
    for k in range(3):
        place = away[PLANE[k][0]] * RING + away[PLANE[k][1]]
        lines.append((away[LINE[k]] * 2 + flip) * 32 + place * 2 + rank[24])
    return table.reshape(-1), jnp.stack(lines)


def on_device(
    fields,
    conv_weight,
    regrid_blocks,
    source_block,
    target_device,
    target_half,
    neighbours,
    hp_weight,
    rate_scale,
):
    channels, lon_cells, lat_cells = fields.shape
    latent_width = conv_weight.shape[1]
    table, lines = routing(source_block, target_device, target_half)
    pre_conv = conv_taps(conv_weight, grid_rims(fields), False)
    hidden = jax.nn.silu(pre_conv).astype(jnp.bfloat16)
    outgoing = spread(lines, hidden, regrid_blocks)
    arrived = line_exchange(outgoing, 1, 0)
    partial = combine(table, arrived)
    codes, *answers = middle(table, neighbours, partial, hp_weight, rate_scale, 1)
    pre_grad = pull(lines, regrid_blocks, pre_conv, answers).reshape(
        latent_width, lon_cells, lat_cells
    )
    grad_fields = conv_taps(conv_weight, grid_rims(pre_grad), True).reshape(
        channels, lon_cells, lat_cells
    )
    return (codes, grad_fields)


def solution(mesh):
    placed = (
        P(None, "lon", "lat"),
        P(),
        P(("lon", "lat"), None, None),
        P(("lon", "lat")),
        P(),
        P(),
        P(("lon", "lat"), None, None),
        P(),
        P(),
    )
    return jax.shard_map(
        on_device,
        mesh=mesh,
        in_specs=placed,
        out_specs=(P(("lon", "lat"), None), P(None, "lon", "lat")),
        check_vma=False,
    )
```

```python
import functools

import jax
import jax.numpy as jnp
from jax import lax
from jax.experimental import pallas as pl
from jax.experimental.pallas import tpu as pltpu
from jax.sharding import PartitionSpec as P

TS = 16
RING = 4
BLOCK = 128
HALVES = 8
GROUP = 8
MESH = pl.DeviceIdType.MESH
LOG_TWO = 0.6931471805599453

PARTS = ((0, 48), (48, 48), (96, 32))
LINE = ("y", "z", "x")
PLANE = (("z", "x"), ("x", "y"), ("y", "z"))


def silu_slope(values):
    sigma = jax.nn.sigmoid(values)
    return sigma * (1.0 + values * (1.0 - sigma))


def laplace_slope(latent, spread):
    inverse = 1.0 / spread
    half_mass = 0.5 * jnp.exp(-0.5 * inverse)
    far = inverse * (1.0 / LOG_TWO)
    scaled = jnp.clip(latent, -0.5, 0.5) * inverse
    grown, shrunk = jnp.exp(scaled), jnp.exp(-scaled)
    slope_near = (half_mass * far) * (grown - shrunk) / (1.0 - half_mass * (grown + shrunk))
    slope_far = jnp.where(latent > 0.0, far, -far)
    return jnp.where(jnp.abs(latent) < 0.5, slope_near, slope_far)


def torus_position():
    lon = lax.axis_index("lon")
    return {"z": lon // 8, "x": (lon // 2) % 4, "c": lon % 2, "y": lax.axis_index("lat")}


def moved(here, **steps):
    place = dict(here)
    for axis, step in steps.items():
        if axis == "c":
            place["c"] = (here["c"] + step) % 2
        else:
            place[axis] = (here[axis] + step + RING) % RING
    return place


def device_at(place):
    return (place["z"] * 8 + place["x"] * 2 + place["c"], place["y"])


def meet(peers):
    barrier = pltpu.get_barrier_semaphore()
    for peer in peers:
        pl.semaphore_signal(barrier, inc=1, device_id=device_at(peer), device_id_type=MESH)
    pl.semaphore_wait(barrier, len(peers))


def line_body(sign, s0, s1, s2, r0, r1, r2, send, recv, local):
    here = torus_position()
    peers = [moved(here, c=1)]
    for axis in LINE:
        for step in range(1, RING):
            for flip in range(2):
                peers.append(moved(here, **{axis: step, "c": flip}))
    meet(peers)
    sources, targets = (s0, s1, s2), (r0, r1, r2)
    copies = []
    for chunk in (4, 5, 2, 3, 6, 7, 1):
        step, flip = chunk // 2, chunk % 2
        for k in range(3):
            copy = pltpu.make_async_remote_copy(
                src_ref=sources[k].at[chunk],
                dst_ref=targets[k].at[chunk],
                send_sem=send.at[k, chunk],
                recv_sem=recv.at[k, chunk],
                device_id=device_at(moved(here, **{LINE[k]: sign * step, "c": flip})),
                device_id_type=MESH,
            )
            copy.start()
            copies.append(copy)
    own = []
    for k in range(3):
        copy = pltpu.make_async_copy(sources[k].at[0], targets[k].at[0], local.at[k])
        copy.start()
        own.append(copy)
    for copy in own + copies:
        copy.wait()


def line_exchange(parts, sign, collective_id):
    anywhere = pl.BlockSpec(memory_space=pl.ANY)
    return pl.pallas_call(
        functools.partial(line_body, sign),
        out_shape=[jax.ShapeDtypeStruct(part.shape, part.dtype) for part in parts],
        in_specs=[anywhere] * 3,
        out_specs=[anywhere] * 3,
        scratch_shapes=[
            pltpu.SemaphoreType.DMA((3, 8)),
            pltpu.SemaphoreType.DMA((3, 8)),
            pltpu.SemaphoreType.DMA((3,)),
        ],
        compiler_params=pltpu.CompilerParams(collective_id=collective_id, has_side_effects=True, vmem_limit_bytes=4 << 20),
        name="line_exchange_%d" % collective_id,
    )(*parts)


def spread_body(table, hidden, blocks, o0, o1, o2, turned):
    outs = (o0, o1, o2)
    for k in range(turned.shape[0]):
        turned[k] = hidden[:, k * BLOCK : (k + 1) * BLOCK].T

    def some(step, carry):
        for b in range(GROUP):
            block = step * GROUP + b
            made = jnp.dot(
                blocks[block], turned[table[0, block]], preferred_element_type=jnp.float32
            ).astype(jnp.bfloat16)
            for k, (start, count) in enumerate(PARTS):
                outs[k][table[1 + k, block]] = made[start : start + count]
        return carry

    lax.fori_loop(0, blocks.shape[0] // GROUP, some, 0)


def spread(table, hidden, regrid_blocks):
    cells, width = regrid_blocks.shape[2], hidden.shape[0]
    vmem = pl.BlockSpec(memory_space=pltpu.VMEM)
    parts = pl.pallas_call(
        spread_body,
        in_specs=[pl.BlockSpec(memory_space=pltpu.SMEM), vmem, vmem],
        out_specs=[vmem] * 3,
        scratch_shapes=[pltpu.VMEM((hidden.shape[1] // BLOCK, cells, width), jnp.bfloat16)],
        out_shape=[jax.ShapeDtypeStruct((256, n, width), jnp.bfloat16) for _, n in PARTS],
        compiler_params=pltpu.CompilerParams(vmem_limit_bytes=24 << 20),
        name="spread",
    )(table, hidden, regrid_blocks)
    return [part.reshape(8, 32, *part.shape[1:]) for part in parts]


def combine_body(table, r0, r1, r2, p0, p1, p2, a0, a1, a2):
    place = pl.program_id(0)
    ins, outs, sums = (r0, r1, r2), (p0, p1, p2), (a0, a1, a2)
    for total in sums:
        total[...] = jnp.zeros_like(total)
    for chunk in range(8):
        for k in range(3):
            entry = k * 256 + chunk * 32 + place * 2
            for rank in range(2):
                half = table[entry + rank]
                sums[k][half] += ins[k][chunk, rank].astype(jnp.float32)
    for k in range(3):
        outs[k][0] = sums[k][:HALVES].astype(jnp.bfloat16)


def combine(table, parts):
    width = parts[0].shape[-1]
    return pl.pallas_call(
        combine_body,
        grid_spec=pltpu.PrefetchScalarGridSpec(
            num_scalar_prefetch=1,
            grid=(16,),
            in_specs=[pl.BlockSpec((8, 2, n, width), lambda i, t: (0, i, 0, 0)) for _, n in PARTS],
            out_specs=[
                pl.BlockSpec((1, HALVES, n, width), lambda i, t: (i, 0, 0, 0)) for _, n in PARTS
            ],
            scratch_shapes=[pltpu.VMEM((HALVES + 1, n, width), jnp.float32) for _, n in PARTS],
        ),
        out_shape=[jax.ShapeDtypeStruct((16, HALVES, n, width), jnp.bfloat16) for _, n in PARTS],
        compiler_params=pltpu.CompilerParams(vmem_limit_bytes=8 << 20),
        name="combine",
    )(table, *parts)


def pull_body(table, blocks, pre_conv, w0, w1, w2, out, sums):
    ins = (w0, w1, w2)
    sums[...] = jnp.zeros_like(sums)

    def some(step, carry):
        for b in range(GROUP):
            block = step * GROUP + b
            grad = jnp.concatenate([ins[k][table[1 + k, block]] for k in range(3)], axis=0)
            sums[table[0, block]] += jnp.dot(
                grad, blocks[block], preferred_element_type=jnp.float32
            )
        return carry

    lax.fori_loop(0, blocks.shape[0] // GROUP, some, 0)
    for k in range(sums.shape[0]):
        cells = slice(k * BLOCK, (k + 1) * BLOCK)
        out[:, cells] = (sums[k] * silu_slope(pre_conv[:, cells])).astype(out.dtype)


def pull(table, regrid_blocks, pre_conv, parts):
    cells, width = regrid_blocks.shape[2], pre_conv.shape[0]
    vmem = pl.BlockSpec(memory_space=pltpu.VMEM)
    return pl.pallas_call(
        pull_body,
        in_specs=[pl.BlockSpec(memory_space=pltpu.SMEM)] + [vmem] * 5,
        out_specs=vmem,
        scratch_shapes=[pltpu.VMEM((pre_conv.shape[1] // BLOCK, width, cells), jnp.float32)],
        out_shape=jax.ShapeDtypeStruct(pre_conv.shape, jnp.bfloat16),
        compiler_params=pltpu.CompilerParams(vmem_limit_bytes=24 << 20),
        name="pull",
    )(table, regrid_blocks, pre_conv, *[part.reshape(256, *part.shape[2:]) for part in parts])


def remote(source, target, send, recv, place):
    copy = pltpu.make_async_remote_copy(
        src_ref=source,
        dst_ref=target,
        send_sem=send,
        recv_sem=recv,
        device_id=place,
        device_id_type=MESH,
    )
    copy.start()
    return copy


def iota(shape, dim):
    return lax.broadcasted_iota(jnp.int32, shape, dim)


def dot(a, b):
    return jnp.dot(a, b, preferred_element_type=jnp.float32)


def dot_turned(a, b):
    return lax.dot_general(a, b, (((1,), (1,)), ((), ())), preferred_element_type=jnp.float32)


def edge_masks(pixels):
    edge, cell = iota((4 * TS, pixels), 0), iota((4 * TS, pixels), 1)
    side, spot = edge >> 4, edge & 15
    wanted = jnp.where(
        side == 0,
        spot,
        jnp.where(side == 1, TS * spot + TS - 1, jnp.where(side == 2, pixels - TS + spot, TS * spot)),
    )
    take_edges = (cell == wanted).astype(jnp.float32).astype(jnp.bfloat16)
    one, other = iota((pixels, pixels), 0), iota((pixels, pixels), 1)
    apart = jnp.abs((one >> 4) - (other >> 4)) + jnp.abs((one & 15) - (other & 15))
    adjacent = (apart == 1).astype(jnp.float32).astype(jnp.bfloat16)
    cell, edge = iota((pixels, 4 * TS), 0), iota((pixels, 4 * TS), 1)
    side, spot = edge >> 4, edge & 15
    row, column = cell >> 4, cell & 15
    along = jnp.where((side & 1) == 0, column, row)
    inward = jnp.where(
        side == 0,
        row,
        jnp.where(side == 1, TS - 1 - column, jnp.where(side == 2, TS - 1 - row, column)),
    )
    return take_edges, adjacent, side, spot, along, inward


def middle_body(
    table, beside, p0, p1, p2, weights, scale, codes, w0, w1, w2,
    a0, a1, a2, b0, b1, b2, c0, c1, c2, latent, grad, edges, rims0, rims1, near_grad,
    u0, u1, u2, v0, v1, v2, first_sems, second_sems, edge_sems, gather_sems, line_sems,
):
    ps, ws, arrived, sums, landed = (p0, p1, p2), (w0, w1, w2), (a0, a1, a2), (b0, b1, b2), (c0, c1, c2)
    us, vs, rims = (u0, u1, u2), (v0, v1, v2), (rims0, rims1)
    here = torus_position()
    lon, lat = lax.axis_index("lon"), lax.axis_index("lat")
    lons, lats = lax.axis_size("lon"), lax.axis_size("lat")
    above, below = (lon + 1) % lons, (lon + lons - 1) % lons
    pixels = TS * TS
    per_tile = pixels // BLOCK
    tiles = latent.shape[0] // per_tile
    columns = [(k, start, count) for k, (start, count) in enumerate(PARTS)]

    barrier = pltpu.get_barrier_semaphore()
    peers = [device_at(moved(here, c=1))]
    for axis in LINE:
        for step in range(1, RING):
            for flip in range(2):
                peers.append(device_at(moved(here, **{axis: step, "c": flip})))
    for step in range(lats):
        row = (lat + step) % lats
        peers += [(above, row), (below, row)]
    for peer in peers:
        pl.semaphore_signal(barrier, inc=1, device_id=peer, device_id_type=MESH)
    pl.semaphore_wait(barrier, len(peers))

    copies = {}
    for step in (2, 1, 3):
        for k in range(3):
            copies[k, step] = remote(
                ps[k].at[:, step],
                arrived[k].at[step],
                first_sems.at[0, k, step],
                first_sems.at[1, k, step],
                device_at(moved(here, **{PLANE[k][1]: step})),
            )
    take_edges, adjacent, side, spot, along, inward = edge_masks(pixels)
    for copy in copies.values():
        copy.wait()
    copies = []
    for step in (2, 1, 3, 0):
        for k in range(3):
            total = ps[k][step, 0].astype(jnp.float32)
            for other in range(1, RING):
                total += arrived[k][other, step].astype(jnp.float32)
            sums[k][step] = total.astype(jnp.bfloat16)
            if step:
                copies.append(
                    remote(
                        sums[k].at[step],
                        landed[k].at[step],
                        second_sems.at[0, k, step],
                        second_sems.at[1, k, step],
                        device_at(moved(here, **{PLANE[k][0]: step})),
                    )
                )
    for copy in copies:
        copy.wait()
    for k, start, count in columns:
        total = sums[k][0].astype(jnp.float32)
        for step in range(1, RING):
            total += landed[k][step].astype(jnp.float32)
        latent[:, start : start + count] = total.astype(jnp.bfloat16)

    def tile_of(values, t):
        return values[t * per_tile : (t + 1) * per_tile].reshape(pixels, values.shape[2])

    def swap(turn, values):
        for t in range(tiles):
            picked = dot(take_edges, tile_of(values, t)).astype(jnp.bfloat16)
            for s in range(4):
                edges[turn, s, t] = picked[s * TS : (s + 1) * TS]
        mine = pl.ds(lat * tiles, tiles)
        sent = []
        for step in (2, 1, 3, 0):
            row = (lat + step) % lats
            ways = [(2, 0, below), (0, 2, above)] + ([(1, 3, lon), (3, 1, lon)] if step else [])
            for from_side, to_side, column in ways:
                sent.append(
                    remote(
                        edges.at[turn, from_side],
                        rims[turn].at[to_side, mine],
                        edge_sems.at[0, turn, to_side, step],
                        edge_sems.at[1, turn, to_side, step],
                        (column, row),
                    )
                )
        rims[turn][3, mine] = edges[turn, 1]
        rims[turn][1, mine] = edges[turn, 3]
        return sent

    def placed(t):
        flips = jnp.zeros_like(side)
        for s in range(4):
            flips = jnp.where(side == s, beside[t * 8 + s * 2 + 1], flips)
        hit = (inward == 0) & (spot == jnp.where(flips == 1, TS - 1 - along, along))
        return hit.astype(jnp.float32).astype(jnp.bfloat16)

    def outer(turn, t, place):
        found = [rims[turn][s, beside[t * 8 + s * 2]] for s in range(4)]
        return dot(place, jnp.concatenate(found, axis=0))

    copies = swap(0, latent)
    places = [placed(t) for t in range(tiles)]
    inner = [dot(adjacent, tile_of(latent, t)) for t in range(tiles)]
    mixes = [dot(tile_of(latent, t), weights[0]) for t in range(tiles)]
    for copy in copies:
        copy.wait()
    mix_grads = []
    for t in range(tiles):
        near_sum = (inner[t] + outer(0, t, places[t])).astype(jnp.bfloat16)
        pre_mix = mixes[t] + dot(near_sum, weights[1])
        mixed = pre_mix * jax.nn.sigmoid(pre_mix)
        codes[t * pixels : (t + 1) * pixels, :] = mixed.astype(jnp.bfloat16)
        mix_grad = (laplace_slope(mixed, scale[...]) * silu_slope(pre_mix)).astype(jnp.bfloat16)
        made = dot_turned(mix_grad, weights[1]).astype(jnp.bfloat16)
        near_grad[t * per_tile : (t + 1) * per_tile] = made.reshape(per_tile, BLOCK, -1)
        mix_grads.append(mix_grad)
    copies = swap(1, near_grad)
    own = [
        dot_turned(mix_grads[t], weights[0]) + dot(adjacent, tile_of(near_grad, t))
        for t in range(tiles)
    ]
    for copy in copies:
        copy.wait()
    for t in range(tiles):
        found = own[t] + outer(1, t, places[t])
        for h in range(per_tile):
            part = found[h * BLOCK : (h + 1) * BLOCK, :]
            grad[t * per_tile + h] = part.T.astype(jnp.bfloat16)

    def gathered(k, source, place, axis, step):
        return remote(
            source,
            us[k].at[place],
            gather_sems.at[0, k, place],
            gather_sems.at[1, k, place],
            device_at(moved(here, **{axis: -step})),
        )

    first, later = {}, []
    mine = [grad.at[:, pl.ds(start, count)] for start, count in PARTS]
    for step in (2, 1, 3):
        for k in range(3):
            first[k, step] = gathered(k, mine[k], step, PLANE[k][1], step)
    for step in (2, 1, 3):
        for k in range(3):
            later.append(gathered(k, mine[k], step * RING, PLANE[k][0], step))
    for k, start, count in columns:
        us[k][0] = grad[:, start : start + count]
    for step in (1, 3, 2):
        for k in range(3):
            first[k, step].wait_recv()
            for hop in (2, 1, 3):
                later.append(gathered(k, us[k].at[step], hop * RING + step, PLANE[k][0], hop))
    for copy in later:
        copy.wait()
    for copy in first.values():
        copy.wait_send()

    copies = []
    for chunk in (4, 5, 2, 3, 6, 7, 1, 0):
        step, flip = chunk // 2, chunk % 2

        def fill(place, carry):
            for k in range(3):
                for rank in range(2):
                    half = jnp.minimum(table[k * 256 + chunk * 32 + place * 2 + rank], HALVES - 1)
                    found = us[k][place, half]
                    if chunk:
                        vs[k][chunk - 1, place * 2 + rank] = found
                    else:
                        ws[k][0, place * 2 + rank] = found
            return carry

        lax.fori_loop(0, RING * RING, fill, 0)
        if chunk:
            for k in range(3):
                copies.append(
                    remote(
                        vs[k].at[chunk - 1],
                        ws[k].at[chunk],
                        line_sems.at[0, k, chunk],
                        line_sems.at[1, k, chunk],
                        device_at(moved(here, **{LINE[k]: -step, "c": flip})),
                    )
                )
    for copy in copies:
        copy.wait()


def middle(table, neighbours, parts, hp_weight, rate_scale, collective_id):
    tiles, width = neighbours.shape[0], hp_weight.shape[1]
    column_tiles = tiles * lax.axis_size("lat")
    pixels = tiles * TS * TS
    beside = jnp.stack([neighbours[:, :, 0] % column_tiles, neighbours[:, :, 2]], axis=-1)
    smem, vmem = pl.BlockSpec(memory_space=pltpu.SMEM), pl.BlockSpec(memory_space=pltpu.VMEM)
    counts = [count for _, count in PARTS]

    def buffers(*lead):
        return [pltpu.VMEM((*lead, n, width), jnp.bfloat16) for n in counts]

    return pl.pallas_call(
        middle_body,
        out_shape=[jax.ShapeDtypeStruct((pixels, width), jnp.bfloat16)]
        + [jax.ShapeDtypeStruct((8, 32, n, width), jnp.bfloat16) for n in counts],
        in_specs=[smem, smem] + [vmem] * 5,
        out_specs=[vmem] * 4,
        scratch_shapes=buffers(RING, RING, HALVES)
        + buffers(RING, HALVES)
        + buffers(RING, HALVES)
        + [
            pltpu.VMEM((HALVES, BLOCK, width), jnp.bfloat16),
            pltpu.VMEM((HALVES, width, BLOCK), jnp.bfloat16),
            pltpu.VMEM((2, 4, tiles, TS, width), jnp.bfloat16),
            pltpu.VMEM((4, column_tiles, TS, width), jnp.bfloat16),
            pltpu.VMEM((4, column_tiles, TS, width), jnp.bfloat16),
            pltpu.VMEM((HALVES, BLOCK, width), jnp.bfloat16),
        ]
        + buffers(RING * RING, HALVES)
        + buffers(7, 32)
        + [
            pltpu.SemaphoreType.DMA((2, 3, RING)),
            pltpu.SemaphoreType.DMA((2, 3, RING)),
            pltpu.SemaphoreType.DMA((2, 2, 4, 4)),
            pltpu.SemaphoreType.DMA((2, 3, RING * RING)),
            pltpu.SemaphoreType.DMA((2, 3, 8)),
        ],
        compiler_params=pltpu.CompilerParams(
            collective_id=collective_id, has_side_effects=True, vmem_limit_bytes=36 << 20
        ),
        name="middle",
    )(
        table,
        beside.reshape(-1),
        *[part.reshape(RING, RING, *part.shape[1:]) for part in parts],
        hp_weight,
        rate_scale.reshape(1, width),
    )


def conv_body(reverse, lon_cells, x, taps, *refs):
    if reverse:
        out, wide, q0, q1, q2, pack, got, sends, recvs = refs
        weight = [taps.at[8 - t] for t in range(9)]
    else:
        out, hidden, wide, q0, q1, q2, pack, got, sends, recvs, turned = refs
        weight = [turned.at[t] for t in range(9)]
    lon, lat = lax.axis_index("lon"), lax.axis_index("lat")
    lons, lats = lax.axis_size("lon"), lax.axis_size("lat")
    above, below = ((lon + 1) % lons, lat), ((lon + lons - 1) % lons, lat)
    north, south = (lon, (lat + 1) % lats), (lon, (lat + lats - 1) % lats)
    barrier = pltpu.get_barrier_semaphore()
    for peer in (above, below, north, south):
        pl.semaphore_signal(barrier, inc=1, device_id=peer, device_id_type=MESH)
    span = lon_cells * BLOCK
    if not reverse:
        for t in range(9):
            turned[t] = taps[t].T
    wide[:, BLOCK : BLOCK + span] = x[...]
    pl.semaphore_wait(barrier, 4)
    rows = [
        remote(
            x.at[:, pl.ds(0, BLOCK)],
            wide.at[:, pl.ds(BLOCK + span, BLOCK)],
            sends.at[0],
            recvs.at[0],
            below,
        ),
        remote(
            x.at[:, pl.ds(span - BLOCK, BLOCK)],
            wide.at[:, pl.ds(0, BLOCK)],
            sends.at[1],
            recvs.at[1],
            above,
        ),
    ]
    shifted = (q0, q1, q2)

    def products(n, offsets):
        for e in offsets:
            total = None
            for a in range(3):
                start = pl.multiple_of(n * 2 * BLOCK + a * BLOCK, BLOCK)
                term = dot(weight[3 * a + e][...], wide[:, pl.ds(start, 2 * BLOCK)])
                total = term if total is None else total + term
            shifted[e][2 * n] = total[:, :BLOCK]
            shifted[e][2 * n + 1] = total[:, BLOCK:]

    pairs = lon_cells // 2

    def inside(n, carry):
        products(n, (0, 1, 2))
        return carry

    lax.fori_loop(1, pairs - 1, inside, 0)
    for copy in rows:
        copy.wait()

    def outside(n, carry):
        products(n * (pairs - 1), (0, 2))
        return carry

    lax.fori_loop(0, 2, outside, 0)
    lane = iota((out.shape[0], BLOCK), 1)
    to_north = jnp.zeros((out.shape[0], BLOCK), jnp.float32)
    to_south = jnp.zeros((out.shape[0], BLOCK), jnp.float32)
    for i in range(lon_cells):
        to_north = jnp.where(lane == i, pltpu.roll(q0[i], i + 1, 1), to_north)
        to_south = jnp.where(lane == i, pltpu.roll(q2[i], i, 1) if i else q2[i], to_south)
    pack[0] = to_north
    pack[1] = to_south
    columns = [
        remote(pack.at[0], got.at[0], sends.at[2], recvs.at[2], north),
        remote(pack.at[1], got.at[1], sends.at[3], recvs.at[3], south),
    ]

    def middle_tap(n, carry):
        products(n * (pairs - 1), (1,))
        return carry

    lax.fori_loop(0, 2, middle_tap, 0)
    for i in range(lon_cells):
        q1[i] = (
            q1[i]
            + jnp.where(lane == 0, 0.0, pltpu.roll(q0[i], 1, 1))
            + jnp.where(lane == BLOCK - 1, 0.0, pltpu.roll(q2[i], BLOCK - 1, 1))
        )
    for copy in columns:
        copy.wait()
    from_south = jnp.where(lat > 0, got[0], 0.0)
    from_north = jnp.where(lat < lats - 1, got[1], 0.0)
    for i in range(lon_cells):
        first = pltpu.roll(from_south, BLOCK - i, 1) if i else from_south
        last = pltpu.roll(from_north, BLOCK - 1 - i, 1)
        value = (
            q1[i] + jnp.where(lane == 0, first, 0.0) + jnp.where(lane == BLOCK - 1, last, 0.0)
        )
        cells = slice(i * BLOCK, (i + 1) * BLOCK)
        out[:, cells] = value
        if not reverse:
            hidden[:, cells] = (value * jax.nn.sigmoid(value)).astype(hidden.dtype)


def grid_conv(cells, taps, reverse, collective_id):
    depth, span = cells.shape
    lon_cells = span // BLOCK
    rows, turned = (taps.shape[1], []) if reverse else (
        taps.shape[2],
        [pltpu.VMEM((9, taps.shape[2], taps.shape[1]), taps.dtype)],
    )
    vmem = pl.BlockSpec(memory_space=pltpu.VMEM)
    shapes = [jax.ShapeDtypeStruct((rows, span), jnp.float32)]
    if not reverse:
        shapes.append(jax.ShapeDtypeStruct((rows, span), jnp.bfloat16))
    return pl.pallas_call(
        functools.partial(conv_body, reverse, lon_cells),
        out_shape=shapes,
        in_specs=[vmem] * 2,
        out_specs=[vmem] * len(shapes),
        scratch_shapes=[pltpu.VMEM((depth, span + 2 * BLOCK), cells.dtype)]
        + [pltpu.VMEM((lon_cells, rows, BLOCK), jnp.float32)] * 3
        + [pltpu.VMEM((2, rows, BLOCK), jnp.float32)] * 2
        + [pltpu.SemaphoreType.DMA((4,)), pltpu.SemaphoreType.DMA((4,))]
        + turned,
        compiler_params=pltpu.CompilerParams(
            collective_id=collective_id, has_side_effects=True, vmem_limit_bytes=24 << 20
        ),
        name="conv_back" if reverse else "conv",
    )(cells, taps)


def routing(source_block, target_device, target_half):
    here = torus_position()
    count = source_block.shape[0]

    def rows_of(values):
        grid = values.reshape(4, 4, 2, 4, count)
        picks = []
        for k in range(3):
            start = [here["z"], here["x"], 0, here["y"], 0]
            size = [1, 1, 2, 1, count]
            at = {"z": 0, "x": 1, "y": 3}[LINE[k]]
            start[at], size[at] = 0, 4
            picks.append(lax.dynamic_slice(grid, start, size).reshape(8, count))
        own = lax.dynamic_slice(
            grid, [here["z"], here["x"], here["c"], here["y"], 0], [1, 1, 1, 1, count]
        )
        return jnp.concatenate(picks + [own.reshape(1, count)], axis=0)

    targets = rows_of(target_device[:, 0])
    halves = rows_of(target_half)[:24]
    ids = jnp.arange(count, dtype=jnp.int32)
    rank = jnp.sum(
        (targets[:, :, None] == targets[:, None, :]) & (ids[None, None, :] < ids[None, :, None]),
        axis=2,
        dtype=jnp.int32,
    )
    to = {"z": targets // 32, "x": (targets // 8) % 4, "c": (targets // 4) % 2, "y": targets % 4}
    codes, order = [], []
    for k in range(3):
        rows = slice(8 * k, 8 * k + 8)
        fits = (to["c"][rows] == here["c"]) & (to[LINE[k]][rows] == here[LINE[k]])
        first, second = [
            (to[axis][rows] - here[axis] + RING) % RING for axis in PLANE[k]
        ]
        codes.append(jnp.where(fits, (first * RING + second) * 2 + rank[rows], -1))
        index = jnp.arange(8, dtype=jnp.int32)
        line, core = (index % RING, index // RING) if k == 0 else (index // 2, index % 2)
        order.append((here[LINE[k]] - line + RING) % RING * 2 + (core + here["c"]) % 2)
    codes = jnp.concatenate(codes, axis=0)
    slots = jnp.arange(32, dtype=jnp.int32)
    found = jnp.sum(
        jnp.where(codes[:, None, :] == slots[None, :, None], (halves - HALVES)[:, None, :], 0),
        axis=2,
    )
    chunk = jnp.arange(8, dtype=jnp.int32)
    table = HALVES + jnp.sum(
        jnp.where(
            jnp.stack(order)[:, None, :, None] == chunk[None, :, None, None],
            found.reshape(3, 1, 8, 32),
            0,
        ),
        axis=2,
    )
    own = {axis: value[24] for axis, value in to.items()}
    away = {axis: (own[axis] - here[axis] + RING) % RING for axis in ("z", "x", "y")}
    flip = (own["c"] + here["c"]) % 2
    lines = [source_block]
    for k in range(3):
        place = away[PLANE[k][0]] * RING + away[PLANE[k][1]]
        lines.append((away[LINE[k]] * 2 + flip) * 32 + place * 2 + rank[24])
    return table.reshape(-1), jnp.stack(lines)


def on_device(
    fields,
    conv_weight,
    regrid_blocks,
    source_block,
    target_device,
    target_half,
    neighbours,
    hp_weight,
    rate_scale,
):
    channels, lon_cells, lat_cells = fields.shape
    table, lines = routing(source_block, target_device, target_half)
    extra = -channels % 16
    taps = jnp.pad(jnp.swapaxes(conv_weight, 1, 2), ((0, 0), (0, extra), (0, 0)))
    columns = jnp.pad(fields.reshape(channels, lon_cells * lat_cells), ((0, extra), (0, 0)))
    pre_conv, hidden = grid_conv(columns, taps, False, 2)
    outgoing = spread(lines, hidden, regrid_blocks)
    arrived = line_exchange(outgoing, 1, 0)
    partial = combine(table, arrived)
    codes, *answers = middle(table, neighbours, partial, hp_weight, rate_scale, 1)
    pre_grad = pull(lines, regrid_blocks, pre_conv, answers)
    (grad_columns,) = grid_conv(pre_grad, taps, True, 3)
    grad_fields = grad_columns[:channels].reshape(channels, lon_cells, lat_cells)
    return (codes, grad_fields)


def solution(mesh):
    placed = (
        P(None, "lon", "lat"),
        P(),
        P(("lon", "lat"), None, None),
        P(("lon", "lat")),
        P(),
        P(),
        P(("lon", "lat"), None, None),
        P(),
        P(),
    )
    return jax.shard_map(
        on_device,
        mesh=mesh,
        in_specs=placed,
        out_specs=(P(("lon", "lat"), None), P(None, "lon", "lat")),
        check_vma=False,
    )
```

```python
import functools

import jax
import jax.numpy as jnp
from jax import lax
from jax.experimental import pallas as pl
from jax.experimental.pallas import tpu as pltpu
from jax.sharding import PartitionSpec as P

TS = 16
RING = 4
BLOCK = 128
HALVES = 8
GROUP = 8
FEW, MANY = 22, 32
MESH = pl.DeviceIdType.MESH
LOG_TWO = 0.6931471805599453

PARTS = ((0, 48), (48, 48), (96, 32))
LINE = ("y", "z", "x")
PLANE = (("z", "x"), ("x", "y"), ("y", "z"))


def silu_slope(values):
    sigma = jax.nn.sigmoid(values)
    return sigma * (1.0 + values * (1.0 - sigma))


def laplace_slope(latent, spread):
    inverse = 1.0 / spread
    half_mass = 0.5 * jnp.exp(-0.5 * inverse)
    far = inverse * (1.0 / LOG_TWO)
    scaled = jnp.clip(latent, -0.5, 0.5) * inverse
    grown, shrunk = jnp.exp(scaled), jnp.exp(-scaled)
    slope_near = (half_mass * far) * (grown - shrunk) / (1.0 - half_mass * (grown + shrunk))
    slope_far = jnp.where(latent > 0.0, far, -far)
    return jnp.where(jnp.abs(latent) < 0.5, slope_near, slope_far)


def torus_position():
    lon = lax.axis_index("lon")
    return {"z": lon // 8, "x": (lon // 2) % 4, "c": lon % 2, "y": lax.axis_index("lat")}


def moved(here, **steps):
    place = dict(here)
    for axis, step in steps.items():
        if axis == "c":
            place["c"] = (here["c"] + step) % 2
        else:
            place[axis] = (here[axis] + step + RING) % RING
    return place


def device_at(place):
    return (place["z"] * 8 + place["x"] * 2 + place["c"], place["y"])


def meet(peers):
    barrier = pltpu.get_barrier_semaphore()
    for peer in peers:
        pl.semaphore_signal(barrier, inc=1, device_id=device_at(peer), device_id_type=MESH)
    pl.semaphore_wait(barrier, len(peers))


def line_body(sign, s0, s1, s2, r0, r1, r2, send, recv, local):
    here = torus_position()
    peers = [moved(here, c=1)]
    for axis in LINE:
        for step in range(1, RING):
            for flip in range(2):
                peers.append(moved(here, **{axis: step, "c": flip}))
    meet(peers)
    sources, targets = (s0, s1, s2), (r0, r1, r2)
    copies = []
    for chunk in (4, 5, 2, 3, 6, 7, 1):
        step, flip = chunk // 2, chunk % 2
        for k in range(3):
            copy = pltpu.make_async_remote_copy(
                src_ref=sources[k].at[chunk],
                dst_ref=targets[k].at[chunk],
                send_sem=send.at[k, chunk],
                recv_sem=recv.at[k, chunk],
                device_id=device_at(moved(here, **{LINE[k]: sign * step, "c": flip})),
                device_id_type=MESH,
            )
            copy.start()
            copies.append(copy)
    own = []
    for k in range(3):
        copy = pltpu.make_async_copy(sources[k].at[0], targets[k].at[0], local.at[k])
        copy.start()
        own.append(copy)
    for copy in own + copies:
        copy.wait()


def line_exchange(parts, sign, collective_id):
    anywhere = pl.BlockSpec(memory_space=pl.ANY)
    return pl.pallas_call(
        functools.partial(line_body, sign),
        out_shape=[jax.ShapeDtypeStruct(part.shape, part.dtype) for part in parts],
        in_specs=[anywhere] * 3,
        out_specs=[anywhere] * 3,
        scratch_shapes=[
            pltpu.SemaphoreType.DMA((3, 8)),
            pltpu.SemaphoreType.DMA((3, 8)),
            pltpu.SemaphoreType.DMA((3,)),
        ],
        compiler_params=pltpu.CompilerParams(collective_id=collective_id, has_side_effects=True, vmem_limit_bytes=4 << 20),
        name="line_exchange_%d" % collective_id,
    )(*parts)


def spread_body(table, hidden, blocks, o0, o1, o2, turned):
    outs = (o0, o1, o2)
    for k in range(turned.shape[0]):
        turned[k] = hidden[:, k * BLOCK : (k + 1) * BLOCK].T

    def some(step, carry):
        for b in range(GROUP):
            block = step * GROUP + b
            made = jnp.dot(
                blocks[block], turned[table[0, block]], preferred_element_type=jnp.float32
            ).astype(jnp.bfloat16)
            for k, (start, count) in enumerate(PARTS):
                spot = table[1 + k, block]
                outs[k][spot >> 5, spot & 31] = made[start : start + count]
        return carry

    lax.fori_loop(0, blocks.shape[0] // GROUP, some, 0)


def spread(table, hidden, regrid_blocks, slots):
    cells, width = regrid_blocks.shape[2], hidden.shape[0]
    vmem = pl.BlockSpec(memory_space=pltpu.VMEM)
    return pl.pallas_call(
        spread_body,
        in_specs=[pl.BlockSpec(memory_space=pltpu.SMEM), vmem, vmem],
        out_specs=[vmem] * 3,
        scratch_shapes=[pltpu.VMEM((hidden.shape[1] // BLOCK, cells, width), jnp.bfloat16)],
        out_shape=[jax.ShapeDtypeStruct((8, slots, n, width), jnp.bfloat16) for _, n in PARTS],
        compiler_params=pltpu.CompilerParams(vmem_limit_bytes=24 << 20),
        name="spread",
    )(table, hidden, regrid_blocks)


def combine_body(table, r0, r1, r2, p0, p1, p2, a0, a1, a2):
    ins, outs, sums = (r0, r1, r2), (p0, p1, p2), (a0, a1, a2)
    places = outs[0].shape[0]

    def clear(place, carry):
        for total in sums:
            cleared = pl.ds(place * HALVES, HALVES)
            total[cleared] = jnp.zeros((HALVES, *total.shape[1:]), jnp.float32)
        return carry

    def add(slot, carry):
        for chunk in range(8):
            for k in range(3):
                spot = table[k * 256 + chunk * 32 + slot]
                sums[k][spot] += ins[k][chunk, slot].astype(jnp.float32)
        return carry

    def give(place, carry):
        for k in range(3):
            outs[k][place] = sums[k][pl.ds(place * HALVES, HALVES)].astype(jnp.bfloat16)
        return carry

    lax.fori_loop(0, places, clear, 0)
    lax.fori_loop(0, ins[0].shape[1], add, 0)
    lax.fori_loop(0, places, give, 0)


def combine(table, parts):
    width = parts[0].shape[-1]
    vmem = pl.BlockSpec(memory_space=pltpu.VMEM)
    return pl.pallas_call(
        combine_body,
        in_specs=[pl.BlockSpec(memory_space=pltpu.SMEM)] + [vmem] * 3,
        out_specs=[vmem] * 3,
        scratch_shapes=[
            pltpu.VMEM((RING * RING * HALVES + 1, n, width), jnp.float32) for _, n in PARTS
        ],
        out_shape=[
            jax.ShapeDtypeStruct((RING * RING, HALVES, n, width), jnp.bfloat16) for _, n in PARTS
        ],
        compiler_params=pltpu.CompilerParams(vmem_limit_bytes=28 << 20),
        name="combine",
    )(table, *parts)


def pull_body(table, blocks, pre_conv, w0, w1, w2, out, sums):
    ins = (w0, w1, w2)
    sums[...] = jnp.zeros_like(sums)

    def some(step, carry):
        for b in range(GROUP):
            block = step * GROUP + b
            spots = [table[1 + k, block] for k in range(3)]
            grad = jnp.concatenate(
                [ins[k][spot >> 5, spot & 31] for k, spot in enumerate(spots)], axis=0
            )
            sums[table[0, block]] += jnp.dot(
                grad, blocks[block], preferred_element_type=jnp.float32
            )
        return carry

    lax.fori_loop(0, blocks.shape[0] // GROUP, some, 0)
    for k in range(sums.shape[0]):
        cells = slice(k * BLOCK, (k + 1) * BLOCK)
        out[:, cells] = (sums[k] * silu_slope(pre_conv[:, cells])).astype(out.dtype)


def pull(table, regrid_blocks, pre_conv, parts):
    cells, width = regrid_blocks.shape[2], pre_conv.shape[0]
    vmem = pl.BlockSpec(memory_space=pltpu.VMEM)
    return pl.pallas_call(
        pull_body,
        in_specs=[pl.BlockSpec(memory_space=pltpu.SMEM)] + [vmem] * 5,
        out_specs=vmem,
        scratch_shapes=[pltpu.VMEM((pre_conv.shape[1] // BLOCK, width, cells), jnp.float32)],
        out_shape=jax.ShapeDtypeStruct(pre_conv.shape, jnp.bfloat16),
        compiler_params=pltpu.CompilerParams(vmem_limit_bytes=24 << 20),
        name="pull",
    )(table, regrid_blocks, pre_conv, *parts)


def remote(source, target, send, recv, place):
    copy = pltpu.make_async_remote_copy(
        src_ref=source,
        dst_ref=target,
        send_sem=send,
        recv_sem=recv,
        device_id=place,
        device_id_type=MESH,
    )
    copy.start()
    return copy


def iota(shape, dim):
    return lax.broadcasted_iota(jnp.int32, shape, dim)


def dot(a, b):
    return jnp.dot(a, b, preferred_element_type=jnp.float32)


def dot_turned(a, b):
    return lax.dot_general(a, b, (((1,), (1,)), ((), ())), preferred_element_type=jnp.float32)


def edge_masks(pixels):
    edge, cell = iota((4 * TS, pixels), 0), iota((4 * TS, pixels), 1)
    side, spot = edge >> 4, edge & 15
    wanted = jnp.where(
        side == 0,
        spot,
        jnp.where(side == 1, TS * spot + TS - 1, jnp.where(side == 2, pixels - TS + spot, TS * spot)),
    )
    take_edges = (cell == wanted).astype(jnp.float32).astype(jnp.bfloat16)
    one, other = iota((pixels, pixels), 0), iota((pixels, pixels), 1)
    apart = jnp.abs((one >> 4) - (other >> 4)) + jnp.abs((one & 15) - (other & 15))
    adjacent = (apart == 1).astype(jnp.float32).astype(jnp.bfloat16)
    cell, edge = iota((pixels, 4 * TS), 0), iota((pixels, 4 * TS), 1)
    side, spot = edge >> 4, edge & 15
    row, column = cell >> 4, cell & 15
    along = jnp.where((side & 1) == 0, column, row)
    inward = jnp.where(
        side == 0,
        row,
        jnp.where(side == 1, TS - 1 - column, jnp.where(side == 2, TS - 1 - row, column)),
    )
    return take_edges, adjacent, side, spot, along, inward


def middle_body(
    table, beside, p0, p1, p2, weights, scale, codes, w0, w1, w2,
    a0, a1, a2, b0, b1, b2, c0, c1, c2, latent, grad, edges, rims0, rims1, near_grad,
    u0, u1, u2, v0, v1, v2, first_sems, second_sems, edge_sems, gather_sems, line_sems,
):
    ps, ws, arrived, sums, landed = (p0, p1, p2), (w0, w1, w2), (a0, a1, a2), (b0, b1, b2), (c0, c1, c2)
    us, vs, rims = (u0, u1, u2), (v0, v1, v2), (rims0, rims1)
    here = torus_position()
    lon, lat = lax.axis_index("lon"), lax.axis_index("lat")
    lons, lats = lax.axis_size("lon"), lax.axis_size("lat")
    above, below = (lon + 1) % lons, (lon + lons - 1) % lons
    pixels = TS * TS
    per_tile = pixels // BLOCK
    tiles = latent.shape[0] // per_tile
    columns = [(k, start, count) for k, (start, count) in enumerate(PARTS)]

    barrier = pltpu.get_barrier_semaphore()
    peers = [device_at(moved(here, c=1))]
    for axis in LINE:
        for step in range(1, RING):
            for flip in range(2):
                peers.append(device_at(moved(here, **{axis: step, "c": flip})))
    for step in range(lats):
        row = (lat + step) % lats
        peers += [(above, row), (below, row)]
    for peer in peers:
        pl.semaphore_signal(barrier, inc=1, device_id=peer, device_id_type=MESH)
    pl.semaphore_wait(barrier, len(peers))

    copies = {}
    for step in (2, 1, 3):
        for k in range(3):
            copies[k, step] = remote(
                ps[k].at[:, step],
                arrived[k].at[step],
                first_sems.at[0, k, step],
                first_sems.at[1, k, step],
                device_at(moved(here, **{PLANE[k][1]: step})),
            )
    take_edges, adjacent, side, spot, along, inward = edge_masks(pixels)
    for copy in copies.values():
        copy.wait()
    copies = []
    for step in (2, 1, 3, 0):
        for k in range(3):
            total = ps[k][step, 0].astype(jnp.float32)
            for other in range(1, RING):
                total += arrived[k][other, step].astype(jnp.float32)
            sums[k][step] = total.astype(jnp.bfloat16)
            if step:
                copies.append(
                    remote(
                        sums[k].at[step],
                        landed[k].at[step],
                        second_sems.at[0, k, step],
                        second_sems.at[1, k, step],
                        device_at(moved(here, **{PLANE[k][0]: step})),
                    )
                )
    for copy in copies:
        copy.wait()
    for k, start, count in columns:
        total = sums[k][0].astype(jnp.float32)
        for step in range(1, RING):
            total += landed[k][step].astype(jnp.float32)
        latent[:, start : start + count] = total.astype(jnp.bfloat16)

    def tile_of(values, t):
        return values[t * per_tile : (t + 1) * per_tile].reshape(pixels, values.shape[2])

    def swap(turn, values):
        for t in range(tiles):
            picked = dot(take_edges, tile_of(values, t)).astype(jnp.bfloat16)
            for s in range(4):
                edges[turn, s, t] = picked[s * TS : (s + 1) * TS]
        mine = pl.ds(lat * tiles, tiles)
        sent = []
        for step in (2, 1, 3, 0):
            row = (lat + step) % lats
            ways = [(2, 0, below), (0, 2, above)] + ([(1, 3, lon), (3, 1, lon)] if step else [])
            for from_side, to_side, column in ways:
                sent.append(
                    remote(
                        edges.at[turn, from_side],
                        rims[turn].at[to_side, mine],
                        edge_sems.at[0, turn, to_side, step],
                        edge_sems.at[1, turn, to_side, step],
                        (column, row),
                    )
                )
        rims[turn][3, mine] = edges[turn, 1]
        rims[turn][1, mine] = edges[turn, 3]
        return sent

    def placed(t):
        flips = jnp.zeros_like(side)
        for s in range(4):
            flips = jnp.where(side == s, beside[t * 8 + s * 2 + 1], flips)
        hit = (inward == 0) & (spot == jnp.where(flips == 1, TS - 1 - along, along))
        return hit.astype(jnp.float32).astype(jnp.bfloat16)

    def outer(turn, t, place):
        found = [rims[turn][s, beside[t * 8 + s * 2]] for s in range(4)]
        return dot(place, jnp.concatenate(found, axis=0))

    copies = swap(0, latent)
    places = [placed(t) for t in range(tiles)]
    inner = [dot(adjacent, tile_of(latent, t)) for t in range(tiles)]
    mixes = [dot(tile_of(latent, t), weights[0]) for t in range(tiles)]
    for copy in copies:
        copy.wait()
    mix_grads = []
    for t in range(tiles):
        near_sum = (inner[t] + outer(0, t, places[t])).astype(jnp.bfloat16)
        pre_mix = mixes[t] + dot(near_sum, weights[1])
        mixed = pre_mix * jax.nn.sigmoid(pre_mix)
        codes[t * pixels : (t + 1) * pixels, :] = mixed.astype(jnp.bfloat16)
        mix_grad = (laplace_slope(mixed, scale[...]) * silu_slope(pre_mix)).astype(jnp.bfloat16)
        made = dot_turned(mix_grad, weights[1]).astype(jnp.bfloat16)
        near_grad[t * per_tile : (t + 1) * per_tile] = made.reshape(per_tile, BLOCK, -1)
        mix_grads.append(mix_grad)
    copies = swap(1, near_grad)
    own = [
        dot_turned(mix_grads[t], weights[0]) + dot(adjacent, tile_of(near_grad, t))
        for t in range(tiles)
    ]
    for copy in copies:
        copy.wait()
    for t in range(tiles):
        found = own[t] + outer(1, t, places[t])
        for h in range(per_tile):
            part = found[h * BLOCK : (h + 1) * BLOCK, :]
            grad[t * per_tile + h] = part.T.astype(jnp.bfloat16)

    def gathered(k, source, place, axis, step):
        return remote(
            source,
            us[k].at[place],
            gather_sems.at[0, k, place],
            gather_sems.at[1, k, place],
            device_at(moved(here, **{axis: -step})),
        )

    first, later = {}, []
    mine = [grad.at[:, pl.ds(start, count)] for start, count in PARTS]
    for step in (2, 1, 3):
        for k in range(3):
            first[k, step] = gathered(k, mine[k], step, PLANE[k][1], step)
    for step in (2, 1, 3):
        for k in range(3):
            later.append(gathered(k, mine[k], step * RING, PLANE[k][0], step))
    for k, start, count in columns:
        us[k][0] = grad[:, start : start + count]
    for step in (1, 3, 2):
        for k in range(3):
            first[k, step].wait_recv()
            for hop in (2, 1, 3):
                later.append(gathered(k, us[k].at[step], hop * RING + step, PLANE[k][0], hop))
    for copy in later:
        copy.wait()
    for copy in first.values():
        copy.wait_send()

    copies = []
    for chunk in (4, 5, 2, 3, 6, 7, 1, 0):
        step, flip = chunk // 2, chunk % 2

        def fill(pair, carry):
            for k in range(3):
                for slot in (2 * pair, 2 * pair + 1):
                    spot = jnp.minimum(
                        table[k * 256 + chunk * 32 + slot], RING * RING * HALVES - 1
                    )
                    found = us[k][spot >> 3, spot & 7]
                    if chunk:
                        vs[k][chunk - 1, slot] = found
                    else:
                        ws[k][0, slot] = found
            return carry

        lax.fori_loop(0, ws[0].shape[1] // 2, fill, 0)
        if chunk:
            for k in range(3):
                copies.append(
                    remote(
                        vs[k].at[chunk - 1],
                        ws[k].at[chunk],
                        line_sems.at[0, k, chunk],
                        line_sems.at[1, k, chunk],
                        device_at(moved(here, **{LINE[k]: -step, "c": flip})),
                    )
                )
    for copy in copies:
        copy.wait()


def middle(table, beside, parts, hp_weight, rate_scale, slots, collective_id):
    tiles, width = beside.shape[0] // 8, hp_weight.shape[1]
    column_tiles = tiles * lax.axis_size("lat")
    pixels = tiles * TS * TS
    smem, vmem = pl.BlockSpec(memory_space=pltpu.SMEM), pl.BlockSpec(memory_space=pltpu.VMEM)
    counts = [count for _, count in PARTS]

    def buffers(*lead):
        return [pltpu.VMEM((*lead, n, width), jnp.bfloat16) for n in counts]

    return pl.pallas_call(
        middle_body,
        out_shape=[jax.ShapeDtypeStruct((pixels, width), jnp.bfloat16)]
        + [jax.ShapeDtypeStruct((8, slots, n, width), jnp.bfloat16) for n in counts],
        in_specs=[smem, smem] + [vmem] * 5,
        out_specs=[vmem] * 4,
        scratch_shapes=buffers(RING, RING, HALVES)
        + buffers(RING, HALVES)
        + buffers(RING, HALVES)
        + [
            pltpu.VMEM((HALVES, BLOCK, width), jnp.bfloat16),
            pltpu.VMEM((HALVES, width, BLOCK), jnp.bfloat16),
            pltpu.VMEM((2, 4, tiles, TS, width), jnp.bfloat16),
            pltpu.VMEM((4, column_tiles, TS, width), jnp.bfloat16),
            pltpu.VMEM((4, column_tiles, TS, width), jnp.bfloat16),
            pltpu.VMEM((HALVES, BLOCK, width), jnp.bfloat16),
        ]
        + buffers(RING * RING, HALVES)
        + buffers(7, slots)
        + [
            pltpu.SemaphoreType.DMA((2, 3, RING)),
            pltpu.SemaphoreType.DMA((2, 3, RING)),
            pltpu.SemaphoreType.DMA((2, 2, 4, 4)),
            pltpu.SemaphoreType.DMA((2, 3, RING * RING)),
            pltpu.SemaphoreType.DMA((2, 3, 8)),
        ],
        compiler_params=pltpu.CompilerParams(
            collective_id=collective_id, has_side_effects=True, vmem_limit_bytes=36 << 20
        ),
        name="middle",
    )(
        table,
        beside,
        *[part.reshape(RING, RING, *part.shape[1:]) for part in parts],
        hp_weight,
        rate_scale.reshape(1, width),
    )


def conv_body(reverse, lon_cells, x, taps, *refs):
    if reverse:
        out, wide, q0, q1, q2, pack, got, sends, recvs = refs
        weight = [taps.at[8 - t] for t in range(9)]
    else:
        out, hidden, wide, q0, q1, q2, pack, got, sends, recvs, turned = refs
        weight = [turned.at[t] for t in range(9)]
    lon, lat = lax.axis_index("lon"), lax.axis_index("lat")
    lons, lats = lax.axis_size("lon"), lax.axis_size("lat")
    above, below = ((lon + 1) % lons, lat), ((lon + lons - 1) % lons, lat)
    north, south = (lon, (lat + 1) % lats), (lon, (lat + lats - 1) % lats)
    barrier = pltpu.get_barrier_semaphore()
    for peer in (above, below, north, south):
        pl.semaphore_signal(barrier, inc=1, device_id=peer, device_id_type=MESH)
    span = lon_cells * BLOCK
    if not reverse:
        for t in range(9):
            turned[t] = taps[t].T
    wide[:, BLOCK : BLOCK + span] = x[...]
    pl.semaphore_wait(barrier, 4)
    rows = [
        remote(
            x.at[:, pl.ds(0, BLOCK)],
            wide.at[:, pl.ds(BLOCK + span, BLOCK)],
            sends.at[0],
            recvs.at[0],
            below,
        ),
        remote(
            x.at[:, pl.ds(span - BLOCK, BLOCK)],
            wide.at[:, pl.ds(0, BLOCK)],
            sends.at[1],
            recvs.at[1],
            above,
        ),
    ]
    shifted = (q0, q1, q2)

    def products(n, offsets):
        for e in offsets:
            total = None
            for a in range(3):
                start = pl.multiple_of(n * 2 * BLOCK + a * BLOCK, BLOCK)
                term = dot(weight[3 * a + e][...], wide[:, pl.ds(start, 2 * BLOCK)])
                total = term if total is None else total + term
            shifted[e][2 * n] = total[:, :BLOCK]
            shifted[e][2 * n + 1] = total[:, BLOCK:]

    pairs = lon_cells // 2

    def inside(n, carry):
        products(n, (0, 1, 2))
        return carry

    lax.fori_loop(1, pairs - 1, inside, 0)
    for copy in rows:
        copy.wait()

    def outside(n, carry):
        products(n * (pairs - 1), (0, 2))
        return carry

    lax.fori_loop(0, 2, outside, 0)
    lane = iota((out.shape[0], BLOCK), 1)
    to_north = jnp.zeros((out.shape[0], BLOCK), jnp.float32)
    to_south = jnp.zeros((out.shape[0], BLOCK), jnp.float32)
    for i in range(lon_cells):
        to_north = jnp.where(lane == i, pltpu.roll(q0[i], i + 1, 1), to_north)
        to_south = jnp.where(lane == i, pltpu.roll(q2[i], i, 1) if i else q2[i], to_south)
    pack[0] = to_north
    pack[1] = to_south
    columns = [
        remote(pack.at[0], got.at[0], sends.at[2], recvs.at[2], north),
        remote(pack.at[1], got.at[1], sends.at[3], recvs.at[3], south),
    ]

    def middle_tap(n, carry):
        products(n * (pairs - 1), (1,))
        return carry

    lax.fori_loop(0, 2, middle_tap, 0)
    for i in range(lon_cells):
        q1[i] = (
            q1[i]
            + jnp.where(lane == 0, 0.0, pltpu.roll(q0[i], 1, 1))
            + jnp.where(lane == BLOCK - 1, 0.0, pltpu.roll(q2[i], BLOCK - 1, 1))
        )
    for copy in columns:
        copy.wait()
    from_south = jnp.where(lat > 0, got[0], 0.0)
    from_north = jnp.where(lat < lats - 1, got[1], 0.0)
    for i in range(lon_cells):
        first = pltpu.roll(from_south, BLOCK - i, 1) if i else from_south
        last = pltpu.roll(from_north, BLOCK - 1 - i, 1)
        value = (
            q1[i] + jnp.where(lane == 0, first, 0.0) + jnp.where(lane == BLOCK - 1, last, 0.0)
        )
        cells = slice(i * BLOCK, (i + 1) * BLOCK)
        out[:, cells] = value
        if not reverse:
            hidden[:, cells] = (value * jax.nn.sigmoid(value)).astype(hidden.dtype)


def grid_conv(cells, taps, reverse, collective_id):
    depth, span = cells.shape
    lon_cells = span // BLOCK
    rows, turned = (taps.shape[1], []) if reverse else (
        taps.shape[2],
        [pltpu.VMEM((9, taps.shape[2], taps.shape[1]), taps.dtype)],
    )
    vmem = pl.BlockSpec(memory_space=pltpu.VMEM)
    shapes = [jax.ShapeDtypeStruct((rows, span), jnp.float32)]
    if not reverse:
        shapes.append(jax.ShapeDtypeStruct((rows, span), jnp.bfloat16))
    return pl.pallas_call(
        functools.partial(conv_body, reverse, lon_cells),
        out_shape=shapes,
        in_specs=[vmem] * 2,
        out_specs=[vmem] * len(shapes),
        scratch_shapes=[pltpu.VMEM((depth, span + 2 * BLOCK), cells.dtype)]
        + [pltpu.VMEM((lon_cells, rows, BLOCK), jnp.float32)] * 3
        + [pltpu.VMEM((2, rows, BLOCK), jnp.float32)] * 2
        + [pltpu.SemaphoreType.DMA((4,)), pltpu.SemaphoreType.DMA((4,))]
        + turned,
        compiler_params=pltpu.CompilerParams(
            collective_id=collective_id, has_side_effects=True, vmem_limit_bytes=24 << 20
        ),
        name="conv_back" if reverse else "conv",
    )(cells, taps)


def routing(source_block, target_device, target_half):
    here = torus_position()
    count = source_block.shape[0]

    def rows_of(values):
        grid = values.reshape(4, 4, 2, 4, count)
        picks = []
        for k in range(3):
            start = [here["z"], here["x"], 0, here["y"], 0]
            size = [1, 1, 2, 1, count]
            at = {"z": 0, "x": 1, "y": 3}[LINE[k]]
            start[at], size[at] = 0, 4
            picks.append(lax.dynamic_slice(grid, start, size).reshape(8, count))
        own = lax.dynamic_slice(
            grid, [here["z"], here["x"], here["c"], here["y"], 0], [1, 1, 1, 1, count]
        )
        return jnp.concatenate(picks + [own.reshape(1, count)], axis=0)

    targets = rows_of(target_device[:, 0])
    halves = rows_of(target_half)[:24]
    ids = jnp.arange(count, dtype=jnp.int32)
    earlier = ids[:, None] < ids[None, :]
    to = {"z": targets // 32, "x": (targets // 8) % 4, "c": (targets // 4) % 2, "y": targets % 4}
    fits, codes, order = [], [], []
    for k in range(3):
        rows = slice(8 * k, 8 * k + 8)
        fits.append((to["c"][rows] == here["c"]) & (to[LINE[k]][rows] == here[LINE[k]]))
        first, second = [(to[axis][rows] - here[axis] + RING) % RING for axis in PLANE[k]]
        codes.append((first * RING + second) * HALVES)
        index = jnp.arange(8, dtype=jnp.int32)
        line, core = (index % RING, index // RING) if k == 0 else (index // 2, index % 2)
        order.append((here[LINE[k]] - line + RING) % RING * 2 + (core + here["c"]) % 2)
    fits = jnp.concatenate(fits, axis=0)
    codes = jnp.concatenate(codes, axis=0) + halves
    turn = jnp.sum((fits[:, :, None] & earlier[None]).astype(jnp.int32), axis=1)
    turn = jnp.where(fits, turn, -1)
    slots = jnp.arange(32, dtype=jnp.int32)
    unused = RING * RING * HALVES
    found = jnp.sum(
        jnp.where(turn[:, None, :] == slots[None, :, None], (codes - unused)[:, None, :], 0),
        axis=2,
    )
    chunk = jnp.arange(8, dtype=jnp.int32)
    table = unused + jnp.sum(
        jnp.where(
            jnp.stack(order)[:, None, :, None] == chunk[None, :, None, None],
            found.reshape(3, 1, 8, 32),
            0,
        ),
        axis=2,
    )
    flip = (to["c"][24] + here["c"]) % 2
    chunks = jnp.stack(
        [(to[axis][24] - here[axis] + RING) % RING * 2 + flip for axis in LINE]
    )
    turns = jnp.sum(
        ((chunks[:, :, None] == chunks[:, None, :]) & earlier[None]).astype(jnp.int32), axis=1
    )
    lines = jnp.concatenate([source_block[None], chunks * 32 + turns], axis=0)
    return table.reshape(-1), lines


def all_fit(target_device, count, slots):
    targets = target_device.reshape(-1, count)
    core = (targets // 4) % 2
    keys = jnp.stack([line * 2 + core for line in (targets % 4, targets // 32, (targets // 8) % 4)])
    words = jnp.arange(3, dtype=jnp.int32)[:, None, None, None]
    marks = jnp.where(keys // 3 == words, jnp.left_shift(1, 10 * (keys % 3)), 0)
    sums = jnp.sum(marks, axis=3)
    counts = jnp.maximum(jnp.maximum(sums & 1023, (sums >> 10) & 1023), sums >> 20)
    return jnp.max(counts) <= slots


def on_device(
    fields,
    conv_weight,
    regrid_blocks,
    source_block,
    target_device,
    target_half,
    neighbours,
    hp_weight,
    rate_scale,
):
    channels, lon_cells, lat_cells = fields.shape
    table, lines = routing(source_block, target_device, target_half)
    extra = -channels % 16
    taps = jnp.pad(jnp.swapaxes(conv_weight, 1, 2), ((0, 0), (0, extra), (0, 0)))
    columns = jnp.pad(fields.reshape(channels, lon_cells * lat_cells), ((0, extra), (0, 0)))
    column_tiles = neighbours.shape[0] * lax.axis_size("lat")
    beside = jnp.stack([neighbours[:, :, 0] % column_tiles, neighbours[:, :, 2]], axis=-1)
    beside = beside.reshape(-1)
    few = all_fit(target_device, source_block.shape[0], FEW)
    pre_conv, hidden = grid_conv(columns, taps, False, 4)

    def step(slots, collective_id):
        outgoing = spread(lines, hidden, regrid_blocks, slots)
        partial = combine(table, line_exchange(outgoing, 1, collective_id))
        codes, *answers = middle(
            table, beside, partial, hp_weight, rate_scale, slots, collective_id + 1
        )
        return codes, pull(lines, regrid_blocks, pre_conv, answers)

    codes, pre_grad = lax.cond(few, lambda: step(FEW, 0), lambda: step(MANY, 2))
    (grad_columns,) = grid_conv(pre_grad, taps, True, 5)
    grad_fields = grad_columns[:channels].reshape(channels, lon_cells, lat_cells)
    return (codes, grad_fields)


def solution(mesh):
    placed = (
        P(None, "lon", "lat"),
        P(),
        P(("lon", "lat"), None, None),
        P(("lon", "lat")),
        P(),
        P(),
        P(("lon", "lat"), None, None),
        P(),
        P(),
    )
    return jax.shard_map(
        on_device,
        mesh=mesh,
        in_specs=placed,
        out_specs=(P(("lon", "lat"), None), P(None, "lon", "lat")),
        check_vma=False,
    )
```

```python
import functools

import jax
import jax.numpy as jnp
from jax import lax
from jax.experimental import pallas as pl
from jax.experimental.pallas import tpu as pltpu
from jax.sharding import PartitionSpec as P

TS = 16
RING = 4
BLOCK = 128
HALVES = 8
GROUP = 8
FEW, MANY = 22, 32
MESH = pl.DeviceIdType.MESH
LOG_TWO = 0.6931471805599453

PARTS = ((0, 48), (48, 48), (96, 32))
LINE = ("y", "z", "x")
PLANE = (("z", "x"), ("x", "y"), ("y", "z"))


def silu_slope(values):
    sigma = jax.nn.sigmoid(values)
    return sigma * (1.0 + values * (1.0 - sigma))


def laplace_slope(latent, spread):
    inverse = 1.0 / spread
    half_mass = 0.5 * jnp.exp(-0.5 * inverse)
    far = inverse * (1.0 / LOG_TWO)
    scaled = jnp.clip(latent, -0.5, 0.5) * inverse
    grown, shrunk = jnp.exp(scaled), jnp.exp(-scaled)
    slope_near = (half_mass * far) * (grown - shrunk) / (1.0 - half_mass * (grown + shrunk))
    slope_far = jnp.where(latent > 0.0, far, -far)
    return jnp.where(jnp.abs(latent) < 0.5, slope_near, slope_far)


def torus_position():
    lon = lax.axis_index("lon")
    return {"z": lon // 8, "x": (lon // 2) % 4, "c": lon % 2, "y": lax.axis_index("lat")}


def moved(here, **steps):
    place = dict(here)
    for axis, step in steps.items():
        if axis == "c":
            place["c"] = (here["c"] + step) % 2
        else:
            place[axis] = (here[axis] + step + RING) % RING
    return place


def device_at(place):
    return (place["z"] * 8 + place["x"] * 2 + place["c"], place["y"])


def meet(peers):
    barrier = pltpu.get_barrier_semaphore()
    for peer in peers:
        pl.semaphore_signal(barrier, inc=1, device_id=device_at(peer), device_id_type=MESH)
    pl.semaphore_wait(barrier, len(peers))


def line_body(sign, s0, s1, s2, r0, r1, r2, send, recv, local):
    here = torus_position()
    peers = [moved(here, c=1)]
    for axis in LINE:
        for step in range(1, RING):
            for flip in range(2):
                peers.append(moved(here, **{axis: step, "c": flip}))
    meet(peers)
    sources, targets = (s0, s1, s2), (r0, r1, r2)
    copies = []
    for chunk in (4, 5, 2, 3, 6, 7, 1):
        step, flip = chunk // 2, chunk % 2
        for k in range(3):
            copy = pltpu.make_async_remote_copy(
                src_ref=sources[k].at[chunk],
                dst_ref=targets[k].at[chunk],
                send_sem=send.at[k, chunk],
                recv_sem=recv.at[k, chunk],
                device_id=device_at(moved(here, **{LINE[k]: sign * step, "c": flip})),
                device_id_type=MESH,
            )
            copy.start()
            copies.append(copy)
    own = []
    for k in range(3):
        copy = pltpu.make_async_copy(sources[k].at[0], targets[k].at[0], local.at[k])
        copy.start()
        own.append(copy)
    for copy in own + copies:
        copy.wait()


def line_exchange(parts, sign, collective_id):
    anywhere = pl.BlockSpec(memory_space=pl.ANY)
    return pl.pallas_call(
        functools.partial(line_body, sign),
        out_shape=[jax.ShapeDtypeStruct(part.shape, part.dtype) for part in parts],
        in_specs=[anywhere] * 3,
        out_specs=[anywhere] * 3,
        scratch_shapes=[
            pltpu.SemaphoreType.DMA((3, 8)),
            pltpu.SemaphoreType.DMA((3, 8)),
            pltpu.SemaphoreType.DMA((3,)),
        ],
        compiler_params=pltpu.CompilerParams(collective_id=collective_id, has_side_effects=True, vmem_limit_bytes=4 << 20),
        name="line_exchange_%d" % collective_id,
    )(*parts)


def spread_body(table, hidden, blocks, o0, o1, o2, turned):
    outs = (o0, o1, o2)
    for k in range(turned.shape[0]):
        turned[k] = hidden[:, k * BLOCK : (k + 1) * BLOCK].T

    def some(step, carry):
        for b in range(GROUP):
            block = step * GROUP + b
            made = jnp.dot(
                blocks[block], turned[table[0, block]], preferred_element_type=jnp.float32
            ).astype(jnp.bfloat16)
            for k, (start, count) in enumerate(PARTS):
                spot = table[1 + k, block]
                outs[k][spot >> 5, spot & 31] = made[start : start + count]
        return carry

    lax.fori_loop(0, blocks.shape[0] // GROUP, some, 0)


def spread(table, hidden, regrid_blocks, slots):
    cells, width = regrid_blocks.shape[2], hidden.shape[0]
    vmem = pl.BlockSpec(memory_space=pltpu.VMEM)
    return pl.pallas_call(
        spread_body,
        in_specs=[pl.BlockSpec(memory_space=pltpu.SMEM), vmem, vmem],
        out_specs=[vmem] * 3,
        scratch_shapes=[pltpu.VMEM((hidden.shape[1] // BLOCK, cells, width), jnp.bfloat16)],
        out_shape=[jax.ShapeDtypeStruct((8, slots, n, width), jnp.bfloat16) for _, n in PARTS],
        compiler_params=pltpu.CompilerParams(vmem_limit_bytes=24 << 20),
        name="spread",
    )(table, hidden, regrid_blocks)


def combine_body(table, r0, r1, r2, p0, p1, p2, a0, a1, a2):
    ins, outs, sums = (r0, r1, r2), (p0, p1, p2), (a0, a1, a2)
    places = outs[0].shape[0]

    def clear(place, carry):
        for total in sums:
            cleared = pl.ds(place * HALVES, HALVES)
            total[cleared] = jnp.zeros((HALVES, *total.shape[1:]), jnp.float32)
        return carry

    def add(slot, carry):
        for chunk in range(8):
            for k in range(3):
                spot = table[k * 8 * BLOCK + chunk * BLOCK + slot]
                sums[k][spot] += ins[k][chunk, slot].astype(jnp.float32)
        return carry

    def give(place, carry):
        for k in range(3):
            outs[k][place] = sums[k][pl.ds(place * HALVES, HALVES)].astype(jnp.bfloat16)
        return carry

    lax.fori_loop(0, places, clear, 0)
    lax.fori_loop(0, ins[0].shape[1], add, 0)
    lax.fori_loop(0, places, give, 0)


def combine(table, parts):
    width = parts[0].shape[-1]
    vmem = pl.BlockSpec(memory_space=pltpu.VMEM)
    return pl.pallas_call(
        combine_body,
        in_specs=[pl.BlockSpec(memory_space=pltpu.SMEM)] + [vmem] * 3,
        out_specs=[vmem] * 3,
        scratch_shapes=[
            pltpu.VMEM((RING * RING * HALVES + 1, n, width), jnp.float32) for _, n in PARTS
        ],
        out_shape=[
            jax.ShapeDtypeStruct((RING * RING, HALVES, n, width), jnp.bfloat16) for _, n in PARTS
        ],
        compiler_params=pltpu.CompilerParams(vmem_limit_bytes=28 << 20),
        name="combine",
    )(table, *parts)


def pull_body(table, blocks, pre_conv, w0, w1, w2, out, sums):
    ins = (w0, w1, w2)
    sums[...] = jnp.zeros_like(sums)

    def some(step, carry):
        for b in range(GROUP):
            block = step * GROUP + b
            spots = [table[1 + k, block] for k in range(3)]
            grad = jnp.concatenate(
                [ins[k][spot >> 5, spot & 31] for k, spot in enumerate(spots)], axis=0
            )
            sums[table[0, block]] += jnp.dot(
                grad, blocks[block], preferred_element_type=jnp.float32
            )
        return carry

    lax.fori_loop(0, blocks.shape[0] // GROUP, some, 0)
    for k in range(sums.shape[0]):
        cells = slice(k * BLOCK, (k + 1) * BLOCK)
        out[:, cells] = (sums[k] * silu_slope(pre_conv[:, cells])).astype(out.dtype)


def pull(table, regrid_blocks, pre_conv, parts):
    cells, width = regrid_blocks.shape[2], pre_conv.shape[0]
    vmem = pl.BlockSpec(memory_space=pltpu.VMEM)
    return pl.pallas_call(
        pull_body,
        in_specs=[pl.BlockSpec(memory_space=pltpu.SMEM)] + [vmem] * 5,
        out_specs=vmem,
        scratch_shapes=[pltpu.VMEM((pre_conv.shape[1] // BLOCK, width, cells), jnp.float32)],
        out_shape=jax.ShapeDtypeStruct(pre_conv.shape, jnp.bfloat16),
        compiler_params=pltpu.CompilerParams(vmem_limit_bytes=24 << 20),
        name="pull",
    )(table, regrid_blocks, pre_conv, *parts)


def remote(source, target, send, recv, place):
    copy = pltpu.make_async_remote_copy(
        src_ref=source,
        dst_ref=target,
        send_sem=send,
        recv_sem=recv,
        device_id=place,
        device_id_type=MESH,
    )
    copy.start()
    return copy


def iota(shape, dim):
    return lax.broadcasted_iota(jnp.int32, shape, dim)


def dot(a, b):
    return jnp.dot(a, b, preferred_element_type=jnp.float32)


def dot_turned(a, b):
    return lax.dot_general(a, b, (((1,), (1,)), ((), ())), preferred_element_type=jnp.float32)


def edge_masks(pixels):
    edge, cell = iota((4 * TS, pixels), 0), iota((4 * TS, pixels), 1)
    side, spot = edge >> 4, edge & 15
    wanted = jnp.where(
        side == 0,
        spot,
        jnp.where(side == 1, TS * spot + TS - 1, jnp.where(side == 2, pixels - TS + spot, TS * spot)),
    )
    take_edges = (cell == wanted).astype(jnp.float32).astype(jnp.bfloat16)
    one, other = iota((pixels, pixels), 0), iota((pixels, pixels), 1)
    apart = jnp.abs((one >> 4) - (other >> 4)) + jnp.abs((one & 15) - (other & 15))
    adjacent = (apart == 1).astype(jnp.float32).astype(jnp.bfloat16)
    cell, edge = iota((pixels, 4 * TS), 0), iota((pixels, 4 * TS), 1)
    side, spot = edge >> 4, edge & 15
    row, column = cell >> 4, cell & 15
    along = jnp.where((side & 1) == 0, column, row)
    inward = jnp.where(
        side == 0,
        row,
        jnp.where(side == 1, TS - 1 - column, jnp.where(side == 2, TS - 1 - row, column)),
    )
    return take_edges, adjacent, side, spot, along, inward


def middle_body(
    table, beside, p0, p1, p2, weights, scale, codes, w0, w1, w2,
    a0, a1, a2, b0, b1, b2, c0, c1, c2, latent, grad, edges, rims0, rims1, near_grad,
    u0, u1, u2, v0, v1, v2, first_sems, second_sems, edge_sems, gather_sems, line_sems,
):
    ps, ws, arrived, sums, landed = (p0, p1, p2), (w0, w1, w2), (a0, a1, a2), (b0, b1, b2), (c0, c1, c2)
    us, vs, rims = (u0, u1, u2), (v0, v1, v2), (rims0, rims1)
    here = torus_position()
    lon, lat = lax.axis_index("lon"), lax.axis_index("lat")
    lons, lats = lax.axis_size("lon"), lax.axis_size("lat")
    above, below = (lon + 1) % lons, (lon + lons - 1) % lons
    pixels = TS * TS
    per_tile = pixels // BLOCK
    tiles = latent.shape[0] // per_tile
    columns = [(k, start, count) for k, (start, count) in enumerate(PARTS)]

    barrier = pltpu.get_barrier_semaphore()
    peers = [device_at(moved(here, c=1))]
    for axis in LINE:
        for step in range(1, RING):
            for flip in range(2):
                peers.append(device_at(moved(here, **{axis: step, "c": flip})))
    for step in range(lats):
        row = (lat + step) % lats
        peers += [(above, row), (below, row)]
    for peer in peers:
        pl.semaphore_signal(barrier, inc=1, device_id=peer, device_id_type=MESH)
    pl.semaphore_wait(barrier, len(peers))

    copies = {}
    for step in (2, 1, 3):
        for k in range(3):
            copies[k, step] = remote(
                ps[k].at[:, step],
                arrived[k].at[step],
                first_sems.at[0, k, step],
                first_sems.at[1, k, step],
                device_at(moved(here, **{PLANE[k][1]: step})),
            )
    take_edges, adjacent, side, spot, along, inward = edge_masks(pixels)
    for copy in copies.values():
        copy.wait()
    copies = []
    for step in (2, 1, 3, 0):
        for k in range(3):
            total = ps[k][step, 0].astype(jnp.float32)
            for other in range(1, RING):
                total += arrived[k][other, step].astype(jnp.float32)
            sums[k][step] = total.astype(jnp.bfloat16)
            if step:
                copies.append(
                    remote(
                        sums[k].at[step],
                        landed[k].at[step],
                        second_sems.at[0, k, step],
                        second_sems.at[1, k, step],
                        device_at(moved(here, **{PLANE[k][0]: step})),
                    )
                )
    for copy in copies:
        copy.wait()
    for k, start, count in columns:
        total = sums[k][0].astype(jnp.float32)
        for step in range(1, RING):
            total += landed[k][step].astype(jnp.float32)
        latent[:, start : start + count] = total.astype(jnp.bfloat16)

    def tile_of(values, t):
        return values[t * per_tile : (t + 1) * per_tile].reshape(pixels, values.shape[2])

    def swap(turn, values):
        for t in range(tiles):
            picked = dot(take_edges, tile_of(values, t)).astype(jnp.bfloat16)
            for s in range(4):
                edges[turn, s, t] = picked[s * TS : (s + 1) * TS]
        mine = pl.ds(lat * tiles, tiles)
        sent = []
        for step in (2, 1, 3, 0):
            row = (lat + step) % lats
            ways = [(2, 0, below), (0, 2, above)] + ([(1, 3, lon), (3, 1, lon)] if step else [])
            for from_side, to_side, column in ways:
                sent.append(
                    remote(
                        edges.at[turn, from_side],
                        rims[turn].at[to_side, mine],
                        edge_sems.at[0, turn, to_side, step],
                        edge_sems.at[1, turn, to_side, step],
                        (column, row),
                    )
                )
        rims[turn][3, mine] = edges[turn, 1]
        rims[turn][1, mine] = edges[turn, 3]
        return sent

    def placed(t):
        flips = jnp.zeros_like(side)
        for s in range(4):
            flips = jnp.where(side == s, beside[t * 8 + s * 2 + 1], flips)
        hit = (inward == 0) & (spot == jnp.where(flips == 1, TS - 1 - along, along))
        return hit.astype(jnp.float32).astype(jnp.bfloat16)

    def outer(turn, t, place):
        found = [rims[turn][s, beside[t * 8 + s * 2]] for s in range(4)]
        return dot(place, jnp.concatenate(found, axis=0))

    copies = swap(0, latent)
    places = [placed(t) for t in range(tiles)]
    inner = [dot(adjacent, tile_of(latent, t)) for t in range(tiles)]
    mixes = [dot(tile_of(latent, t), weights[0]) for t in range(tiles)]
    for copy in copies:
        copy.wait()
    mix_grads = []
    for t in range(tiles):
        near_sum = (inner[t] + outer(0, t, places[t])).astype(jnp.bfloat16)
        pre_mix = mixes[t] + dot(near_sum, weights[1])
        mixed = pre_mix * jax.nn.sigmoid(pre_mix)
        codes[t * pixels : (t + 1) * pixels, :] = mixed.astype(jnp.bfloat16)
        mix_grad = (laplace_slope(mixed, scale[...]) * silu_slope(pre_mix)).astype(jnp.bfloat16)
        made = dot_turned(mix_grad, weights[1]).astype(jnp.bfloat16)
        near_grad[t * per_tile : (t + 1) * per_tile] = made.reshape(per_tile, BLOCK, -1)
        mix_grads.append(mix_grad)
    copies = swap(1, near_grad)
    own = [
        dot_turned(mix_grads[t], weights[0]) + dot(adjacent, tile_of(near_grad, t))
        for t in range(tiles)
    ]
    for copy in copies:
        copy.wait()
    for t in range(tiles):
        found = own[t] + outer(1, t, places[t])
        for h in range(per_tile):
            part = found[h * BLOCK : (h + 1) * BLOCK, :]
            grad[t * per_tile + h] = part.T.astype(jnp.bfloat16)

    def gathered(k, source, place, axis, step):
        return remote(
            source,
            us[k].at[place],
            gather_sems.at[0, k, place],
            gather_sems.at[1, k, place],
            device_at(moved(here, **{axis: -step})),
        )

    first, later = {}, []
    mine = [grad.at[:, pl.ds(start, count)] for start, count in PARTS]
    for step in (2, 1, 3):
        for k in range(3):
            first[k, step] = gathered(k, mine[k], step, PLANE[k][1], step)
    for step in (2, 1, 3):
        for k in range(3):
            later.append(gathered(k, mine[k], step * RING, PLANE[k][0], step))
    for k, start, count in columns:
        us[k][0] = grad[:, start : start + count]
    for step in (1, 3, 2):
        for k in range(3):
            first[k, step].wait_recv()
            for hop in (2, 1, 3):
                later.append(gathered(k, us[k].at[step], hop * RING + step, PLANE[k][0], hop))
    for copy in later:
        copy.wait()
    for copy in first.values():
        copy.wait_send()

    copies = []
    for chunk in (4, 5, 2, 3, 6, 7, 1, 0):
        step, flip = chunk // 2, chunk % 2

        def fill(pair, carry):
            for k in range(3):
                for slot in (2 * pair, 2 * pair + 1):
                    spot = jnp.minimum(
                        table[k * 8 * BLOCK + chunk * BLOCK + slot], RING * RING * HALVES - 1
                    )
                    found = us[k][spot >> 3, spot & 7]
                    if chunk:
                        vs[k][chunk - 1, slot] = found
                    else:
                        ws[k][0, slot] = found
            return carry

        lax.fori_loop(0, ws[0].shape[1] // 2, fill, 0)
        if chunk:
            for k in range(3):
                copies.append(
                    remote(
                        vs[k].at[chunk - 1],
                        ws[k].at[chunk],
                        line_sems.at[0, k, chunk],
                        line_sems.at[1, k, chunk],
                        device_at(moved(here, **{LINE[k]: -step, "c": flip})),
                    )
                )
    for copy in copies:
        copy.wait()


def middle(table, beside, parts, hp_weight, rate_scale, slots, collective_id):
    tiles, width = beside.shape[0] // 8, hp_weight.shape[1]
    column_tiles = tiles * lax.axis_size("lat")
    pixels = tiles * TS * TS
    smem, vmem = pl.BlockSpec(memory_space=pltpu.SMEM), pl.BlockSpec(memory_space=pltpu.VMEM)
    counts = [count for _, count in PARTS]

    def buffers(*lead):
        return [pltpu.VMEM((*lead, n, width), jnp.bfloat16) for n in counts]

    return pl.pallas_call(
        middle_body,
        out_shape=[jax.ShapeDtypeStruct((pixels, width), jnp.bfloat16)]
        + [jax.ShapeDtypeStruct((8, slots, n, width), jnp.bfloat16) for n in counts],
        in_specs=[smem, smem] + [vmem] * 5,
        out_specs=[vmem] * 4,
        scratch_shapes=buffers(RING, RING, HALVES)
        + buffers(RING, HALVES)
        + buffers(RING, HALVES)
        + [
            pltpu.VMEM((HALVES, BLOCK, width), jnp.bfloat16),
            pltpu.VMEM((HALVES, width, BLOCK), jnp.bfloat16),
            pltpu.VMEM((2, 4, tiles, TS, width), jnp.bfloat16),
            pltpu.VMEM((4, column_tiles, TS, width), jnp.bfloat16),
            pltpu.VMEM((4, column_tiles, TS, width), jnp.bfloat16),
            pltpu.VMEM((HALVES, BLOCK, width), jnp.bfloat16),
        ]
        + buffers(RING * RING, HALVES)
        + buffers(7, slots)
        + [
            pltpu.SemaphoreType.DMA((2, 3, RING)),
            pltpu.SemaphoreType.DMA((2, 3, RING)),
            pltpu.SemaphoreType.DMA((2, 2, 4, 4)),
            pltpu.SemaphoreType.DMA((2, 3, RING * RING)),
            pltpu.SemaphoreType.DMA((2, 3, 8)),
        ],
        compiler_params=pltpu.CompilerParams(
            collective_id=collective_id, has_side_effects=True, vmem_limit_bytes=36 << 20
        ),
        name="middle",
    )(
        table,
        beside,
        *[part.reshape(RING, RING, *part.shape[1:]) for part in parts],
        hp_weight,
        rate_scale.reshape(1, width),
    )


def conv_body(reverse, lon_cells, x, taps, *refs):
    if reverse:
        out, wide, q0, q1, q2, pack, got, sends, recvs = refs
        weight = [taps.at[8 - t] for t in range(9)]
    else:
        out, hidden, wide, q0, q1, q2, pack, got, sends, recvs, turned = refs
        weight = [turned.at[t] for t in range(9)]
    lon, lat = lax.axis_index("lon"), lax.axis_index("lat")
    lons, lats = lax.axis_size("lon"), lax.axis_size("lat")
    above, below = ((lon + 1) % lons, lat), ((lon + lons - 1) % lons, lat)
    north, south = (lon, (lat + 1) % lats), (lon, (lat + lats - 1) % lats)
    barrier = pltpu.get_barrier_semaphore()
    for peer in (above, below, north, south):
        pl.semaphore_signal(barrier, inc=1, device_id=peer, device_id_type=MESH)
    span = lon_cells * BLOCK
    if not reverse:
        for t in range(9):
            turned[t] = taps[t].T
    wide[:, BLOCK : BLOCK + span] = x[...]
    pl.semaphore_wait(barrier, 4)
    rows = [
        remote(
            x.at[:, pl.ds(0, BLOCK)],
            wide.at[:, pl.ds(BLOCK + span, BLOCK)],
            sends.at[0],
            recvs.at[0],
            below,
        ),
        remote(
            x.at[:, pl.ds(span - BLOCK, BLOCK)],
            wide.at[:, pl.ds(0, BLOCK)],
            sends.at[1],
            recvs.at[1],
            above,
        ),
    ]
    shifted = (q0, q1, q2)

    def products(n, offsets):
        for e in offsets:
            total = None
            for a in range(3):
                start = pl.multiple_of(n * 2 * BLOCK + a * BLOCK, BLOCK)
                term = dot(weight[3 * a + e][...], wide[:, pl.ds(start, 2 * BLOCK)])
                total = term if total is None else total + term
            shifted[e][2 * n] = total[:, :BLOCK]
            shifted[e][2 * n + 1] = total[:, BLOCK:]

    pairs = lon_cells // 2

    def inside(n, carry):
        products(n, (0, 1, 2))
        return carry

    lax.fori_loop(1, pairs - 1, inside, 0)
    for copy in rows:
        copy.wait()

    def outside(n, carry):
        products(n * (pairs - 1), (0, 2))
        return carry

    lax.fori_loop(0, 2, outside, 0)
    lane = iota((out.shape[0], BLOCK), 1)
    to_north = jnp.zeros((out.shape[0], BLOCK), jnp.float32)
    to_south = jnp.zeros((out.shape[0], BLOCK), jnp.float32)
    for i in range(lon_cells):
        to_north = jnp.where(lane == i, pltpu.roll(q0[i], i + 1, 1), to_north)
        to_south = jnp.where(lane == i, pltpu.roll(q2[i], i, 1) if i else q2[i], to_south)
    pack[0] = to_north
    pack[1] = to_south
    columns = [
        remote(pack.at[0], got.at[0], sends.at[2], recvs.at[2], north),
        remote(pack.at[1], got.at[1], sends.at[3], recvs.at[3], south),
    ]

    def middle_tap(n, carry):
        products(n * (pairs - 1), (1,))
        return carry

    lax.fori_loop(0, 2, middle_tap, 0)
    for i in range(lon_cells):
        q1[i] = (
            q1[i]
            + jnp.where(lane == 0, 0.0, pltpu.roll(q0[i], 1, 1))
            + jnp.where(lane == BLOCK - 1, 0.0, pltpu.roll(q2[i], BLOCK - 1, 1))
        )
    for copy in columns:
        copy.wait()
    from_south = jnp.where(lat > 0, got[0], 0.0)
    from_north = jnp.where(lat < lats - 1, got[1], 0.0)
    for i in range(lon_cells):
        first = pltpu.roll(from_south, BLOCK - i, 1) if i else from_south
        last = pltpu.roll(from_north, BLOCK - 1 - i, 1)
        value = (
            q1[i] + jnp.where(lane == 0, first, 0.0) + jnp.where(lane == BLOCK - 1, last, 0.0)
        )
        cells = slice(i * BLOCK, (i + 1) * BLOCK)
        out[:, cells] = value
        if not reverse:
            hidden[:, cells] = (value * jax.nn.sigmoid(value)).astype(hidden.dtype)


def grid_conv(cells, taps, reverse, collective_id):
    depth, span = cells.shape
    lon_cells = span // BLOCK
    rows, turned = (taps.shape[1], []) if reverse else (
        taps.shape[2],
        [pltpu.VMEM((9, taps.shape[2], taps.shape[1]), taps.dtype)],
    )
    vmem = pl.BlockSpec(memory_space=pltpu.VMEM)
    shapes = [jax.ShapeDtypeStruct((rows, span), jnp.float32)]
    if not reverse:
        shapes.append(jax.ShapeDtypeStruct((rows, span), jnp.bfloat16))
    return pl.pallas_call(
        functools.partial(conv_body, reverse, lon_cells),
        out_shape=shapes,
        in_specs=[vmem] * 2,
        out_specs=[vmem] * len(shapes),
        scratch_shapes=[pltpu.VMEM((depth, span + 2 * BLOCK), cells.dtype)]
        + [pltpu.VMEM((lon_cells, rows, BLOCK), jnp.float32)] * 3
        + [pltpu.VMEM((2, rows, BLOCK), jnp.float32)] * 2
        + [pltpu.SemaphoreType.DMA((4,)), pltpu.SemaphoreType.DMA((4,))]
        + turned,
        compiler_params=pltpu.CompilerParams(
            collective_id=collective_id, has_side_effects=True, vmem_limit_bytes=24 << 20
        ),
        name="conv_back" if reverse else "conv",
    )(cells, taps)


def routing_body(targets, halves, sources, table, lines, most, rows_t, rows_h):
    here = torus_position()
    for k in range(3):
        for chunk in range(8):
            lon, lat = device_at(moved(here, **{LINE[k]: -(chunk // 2), "c": chunk % 2}))
            row = pl.ds(lon * RING + lat, 1)
            rows_t[8 * k + chunk : 8 * k + chunk + 1, :] = targets[row, :]
            rows_h[8 * k + chunk : 8 * k + chunk + 1, :] = halves[row, :]
    shape = rows_t.shape
    part, lane = iota(shape, 0) >> 3, iota(shape, 1)

    def coordinates(t):
        return {"z": t >> 5, "x": (t >> 3) & 3, "c": (t >> 2) & 1, "y": t & 3}

    def by_part(values, axes):
        return jnp.where(
            part == 0, values[axes[0]], jnp.where(part == 1, values[axes[1]], values[axes[2]])
        )

    def away(values, axes):
        return (by_part(values, axes) - by_part(here, axes) + RING) & 3

    def ones(mask):
        return mask.astype(jnp.float32).astype(jnp.bfloat16)

    size = shape[1]
    earlier = ones(iota((size, size), 0) < iota((size, size), 1))
    to = coordinates(rows_t[...])
    firsts, seconds = [axes[0] for axes in PLANE], [axes[1] for axes in PLANE]
    code = (away(to, firsts) * RING + away(to, seconds)) * HALVES + rows_h[...]
    fits = (to["c"] == here["c"]) & (away(to, LINE) == 0)
    turn = jnp.where(fits, dot(ones(fits), earlier), -1.0)
    unused = RING * RING * HALVES
    value = (code - unused).astype(jnp.float32)
    found = jnp.full(shape, float(unused), jnp.float32)
    for slot in range(MANY):
        picked = jnp.sum(jnp.where(turn == slot, value, 0.0), axis=1, keepdims=True)
        found += jnp.where(lane == slot, picked, 0.0)
    table[...] = found.astype(jnp.int32)

    own = coordinates(jnp.broadcast_to(rows_t[0:1, :], shape))
    chunk = away(own, LINE) * 2 + jnp.where(own["c"] == here["c"], 0, 1)
    group = iota(shape, 0) & 7
    mine = chunk == group
    spot = jnp.where(mine, group.astype(jnp.float32) * MANY + dot(ones(mine), earlier), 0.0)
    lines[0:1, :] = sources[...]
    for k in range(3):
        lines[k + 1 : k + 2, :] = jnp.sum(
            spot[8 * k : 8 * k + 8, :], axis=0, keepdims=True
        ).astype(jnp.int32)

    everyone = coordinates(targets[...])
    largest = jnp.zeros((targets.shape[0], 1), jnp.float32)
    for axis in LINE:
        keys = everyone[axis] * 2 + everyone["c"]
        for key in range(8):
            held = jnp.sum((keys == key).astype(jnp.float32), axis=1, keepdims=True)
            largest = jnp.maximum(largest, held)
    most[...] = jnp.broadcast_to(jnp.max(largest, axis=0, keepdims=True), most.shape).astype(
        jnp.int32
    )


def routing(source_block, target_device, target_half):
    count = source_block.shape[0]
    vmem = pl.BlockSpec(memory_space=pltpu.VMEM)
    table, lines, most = pl.pallas_call(
        routing_body,
        in_specs=[vmem] * 3,
        out_specs=[vmem] * 3,
        out_shape=[
            jax.ShapeDtypeStruct((24, count), jnp.int32),
            jax.ShapeDtypeStruct((4, count), jnp.int32),
            jax.ShapeDtypeStruct((8, count), jnp.int32),
        ],
        scratch_shapes=[pltpu.VMEM((24, count), jnp.int32)] * 2,
        compiler_params=pltpu.CompilerParams(vmem_limit_bytes=8 << 20),
        name="routing",
    )(
        target_device.reshape(-1, count),
        target_half.reshape(-1, count),
        source_block.reshape(1, count),
    )
    return table.reshape(-1), lines, most[0, 0]


def on_device(
    fields,
    conv_weight,
    regrid_blocks,
    source_block,
    target_device,
    target_half,
    neighbours,
    hp_weight,
    rate_scale,
):
    channels, lon_cells, lat_cells = fields.shape
    table, lines, most = routing(source_block, target_device, target_half)
    extra = -channels % 16
    taps = jnp.pad(jnp.swapaxes(conv_weight, 1, 2), ((0, 0), (0, extra), (0, 0)))
    columns = jnp.pad(fields.reshape(channels, lon_cells * lat_cells), ((0, extra), (0, 0)))
    column_tiles = neighbours.shape[0] * lax.axis_size("lat")
    beside = jnp.stack([neighbours[:, :, 0] % column_tiles, neighbours[:, :, 2]], axis=-1)
    beside = beside.reshape(-1)
    pre_conv, hidden = grid_conv(columns, taps, False, 4)

    def step(slots, collective_id):
        outgoing = spread(lines, hidden, regrid_blocks, slots)
        partial = combine(table, line_exchange(outgoing, 1, collective_id))
        codes, *answers = middle(
            table, beside, partial, hp_weight, rate_scale, slots, collective_id + 1
        )
        return codes, pull(lines, regrid_blocks, pre_conv, answers)

    codes, pre_grad = lax.cond(most <= FEW, lambda: step(FEW, 0), lambda: step(MANY, 2))
    (grad_columns,) = grid_conv(pre_grad, taps, True, 5)
    grad_fields = grad_columns[:channels].reshape(channels, lon_cells, lat_cells)
    return (codes, grad_fields)


def solution(mesh):
    placed = (
        P(None, "lon", "lat"),
        P(),
        P(("lon", "lat"), None, None),
        P(("lon", "lat")),
        P(),
        P(),
        P(("lon", "lat"), None, None),
        P(),
        P(),
    )
    return jax.shard_map(
        on_device,
        mesh=mesh,
        in_specs=placed,
        out_specs=(P(("lon", "lat"), None), P(None, "lon", "lat")),
        check_vma=False,
    )
```
